512 devices in a mesh: blade: 4 (over z_hi), grid: 128 (over y, z_lo, x, core).
Axes of the slice: x: 4, y: 8, z: 8 (z_hi: 4, z_lo: 2; z = z_hi * 2 + z_lo), core: 2. Of those that a mesh axis runs over, the one named last changes fastest.
Arguments:
- modal_blocks: float32 [4, 3072, 3, 16, 128], P('blade', 'grid'), may hold values from -4 to 4
- amplitudes: float32 [4, 24], P('blade'), may hold values from 0.2 to 1
- owner_map: int32 [4], P('blade'), may hold values from 0 to 127
- span_interp: float32 [4, 16, 4096], P('blade', None, 'grid'), may hold values from -1.5 to 1.5
- chord_interp: float32 [4, 16384, 256], P('blade', 'grid'), may hold values from -0.5 to 0.5
- base_coords: float32 [4, 3, 4096, 256], P('blade', None, 'grid'), may hold values from -6 to 6
- flow_state: float32 [4, 3, 4096, 256], P('blade', None, 'grid'), may hold values from -6 to 6
- face_rows: int32 [4, 12288], P('blade', 'grid'), may hold values from 0 to 31
- face_owner: int32 [4, 12288, 1], P('blade', 'grid'), may hold values from 0 to 127; in each aligned block of 96 rows (0 to 95, 96 to 191, ..., all dimensions but the last counted through in order) at most 2 rows name the same one
Outputs:
- residual: float32 [4, 4096, 256], P('blade', 'grid')
- fringe_faces: float32 [4, 32768, 3, 256], P('blade', 'grid')
The draws below stay inside these ranges and needn't reach their ends.
Inputs may be any that keep to these rules, and one draw needn't show every extreme that they name: `face_owner`: in the 96 faces of one grid block, no receiver is named more than 2 times, and some block names one receiver exactly 2 times.
All inputs are finite; a program needn't handle non-finite values.
Results may differ from the reference program's by a relative error of at most 0.0003.
Values sent between devices are 32-bit elements; how exact they have to be, the bound alone decides.
A program may use at most 64 MiB of HBM per device.

```python
import math
import jax
import jax.numpy as jnp
import numpy as np
from jax import lax

BLADES = 4
MODES = 24
SI = 16
SJ = 128
LI = 32
LJ = 256
CAP = 2
NF = 96
N_GRID = 128


def with_ends(array, stream_key, low, largest):
    index_at = [jax.random.randint(jax.random.fold_in(stream_key, axis), (), 0, length) for axis, length in enumerate(array.shape)]
    widest = array.shape.index(max(array.shape))
    beside = index_at[:widest] + [(index_at[widest] + 1) % array.shape[widest]] + index_at[widest + 1:]
    return array.at[tuple(index_at)].set(low).at[tuple(beside)].set(largest)


def shard_levels(key, shape, pieces, least, largest):
    def one(dim, blocks):
        heights = jax.random.uniform(jax.random.fold_in(jax.random.fold_in(key, 6), dim), (blocks,), jnp.float32, least / len(pieces), largest / len(pieces))
        return jnp.repeat(jnp.exp(heights), shape[dim] // blocks).reshape((-1,) + (1,) * (len(shape) - dim - 1))

    level = one(*pieces[0])
    for cut in pieces[1:]:
        level = level * one(*cut)
    return level


def assign_block(key, own, number, rows, amount, top, reach, slope):
    order = jax.random.permutation(key, amount)
    crowded, usual = shares(amount, rows * top, reach, slope, True), shares(amount, rows * top, reach, slope, False)
    places = jnp.arange(amount)

    def named(sizes, offset_by):
        used = int((sizes > 0).sum())
        fixed = max(1, used // 4)
        moved = fixed + (places - fixed + offset_by * (used - fixed)) % max(1, amount - fixed)
        return jnp.zeros((amount,), jnp.int32).at[order[jnp.where(places < fixed, places, moved)]].set(jnp.asarray(sizes, jnp.int32))

    sizes = jnp.where(number % 4 == 0, named(crowded, number // 4), named(usual, number - number // 4 - 1))
    mixed = jax.random.permutation(jax.random.fold_in(own, 3), amount)
    giver, taker = mixed[0:amount // 2 * 2:2], mixed[1:amount // 2 * 2:2]
    margin = jnp.minimum(sizes[giver] - 1, reach - sizes[taker]) // 2
    margin = jnp.where((giver == order[0]) | (taker == order[0]) | (sizes[taker] == 0), 0, jnp.maximum(margin, 0))
    moved = jax.random.randint(jax.random.fold_in(own, 4), (amount // 2,), 0, 1 << 20) % (margin + 1)
    sizes = sizes.at[giver].add(-moved).at[taker].add(moved)
    members = jnp.searchsorted(jnp.cumsum(sizes), jnp.arange(rows * top), side="right").astype(jnp.int32)
    grid = members.reshape(top, rows).T
    grid = grid[jax.random.permutation(jax.random.fold_in(own, 1), rows)]
    offset_by = jax.random.randint(jax.random.fold_in(own, 2), (rows, 1), 0, top)
    return jnp.take_along_axis(grid, (jnp.arange(top)[None, :] + offset_by) % top, axis=1)


def shares(amount, total, reach, slope, full):
    weights = [(1 << 20) // math.isqrt(grade ** slope) + 1 for grade in range(1, amount + 1)]
    largest = reach if full else min(reach, max(-(-total // amount), total * weights[0] // sum(weights)))
    least = 1 if total - largest >= amount - 1 else 0
    given, rest = [largest] + [least] * (amount - 1), total - largest - least * (amount - 1)
    while rest > 0:
        free = [i for i in range(1, amount) if given[i] < largest] or [i for i in range(1, amount) if given[i] < reach]
        whole, budget = sum([weights[i] for i in free]), rest
        for i in free:
            addition = min(reach - given[i], max(1, budget * weights[i] // whole), rest)
            given[i] = given[i] + addition
            rest = rest - addition
    return np.array(given)


def scatter_about(rng, dims, spread, reach, split=(), kind=jnp.bfloat16):
    values = jax.random.normal(rng, dims, jnp.float32) * spread
    if len(split) > 0:
        values = shard_levels(rng, dims, split, -0.22, 0.18) * values
    return jnp.clip(values, min=-reach, max=reach).astype(kind)


def setup_inputs(seed: int = 0) -> dict:
    streams_of = jax.random.split(jax.random.key(seed), 10)
    modal_blocks = scatter_about(streams_of[0], (BLADES, N_GRID * MODES, 3, SI, SJ), 0.3, 4.0, ((0, 4), (1, 128)), jnp.float32)
    amplitudes = jnp.clip(jnp.exp(math.log(1.0) - 1.609438 * jax.random.uniform(streams_of[1], (BLADES, MODES), jnp.float32) ** shard_levels(streams_of[1], (BLADES, MODES), ((0, 4),), -0.2, 0.2)), 0.2, 1.0)
    owner_map = with_ends(jax.random.randint(streams_of[2], (BLADES,), 0, N_GRID), jax.random.fold_in(streams_of[2], 1), 0, N_GRID - 1).astype(jnp.int32)
    span_interp = scatter_about(streams_of[3], (BLADES, SI, N_GRID * LI), SI ** -0.5, 1.5, ((0, 4), (2, 128)), jnp.float32)
    chord_interp = scatter_about(streams_of[4], (BLADES, N_GRID * SJ, LJ), SJ ** -0.5, 0.5, ((0, 4), (1, 128)), jnp.float32)
    base_coords = scatter_about(streams_of[5], (BLADES, 3, N_GRID * LI, LJ), 1.0, 6.0, ((0, 4), (2, 128)), jnp.float32)
    flow_state = scatter_about(streams_of[6], (BLADES, 3, N_GRID * LI, LJ), 1.0, 6.0, ((0, 4), (2, 128)), jnp.float32)
    face_rows = with_ends(jax.random.randint(streams_of[7], (BLADES, N_GRID * NF), 0, LI), jax.random.fold_in(streams_of[7], 1), 0, LI - 1).astype(jnp.int32)
    face_owner_keys = jax.random.split(jax.random.fold_in(streams_of[8], 1), BLADES * (N_GRID * NF) // NF)
    face_owner_turns = jax.random.permutation(jax.random.fold_in(streams_of[8], 3), BLADES * (N_GRID * NF) // NF)
    face_owner = jax.vmap(lambda own, number: assign_block(jax.random.fold_in(streams_of[8], 2), own, number, NF, N_GRID, 1, CAP, 2))(face_owner_keys, face_owner_turns).reshape((BLADES, N_GRID * NF, 1))
    return dict(modal_blocks=modal_blocks, amplitudes=amplitudes, owner_map=owner_map, span_interp=span_interp, chord_interp=chord_interp, base_coords=base_coords, flow_state=flow_state, face_rows=face_rows, face_owner=face_owner)


ALPHA_SIDE = 1.0 / 3.0
FIRST_COEF = 7.0 / 9.0
SECOND_COEF = 1.0 / 36.0

def compact_operator(count):
    positions = jnp.arange(count)
    offset = positions[None, :] - positions[:, None]
    bmatrix = (jnp.where(offset == 1, FIRST_COEF, 0.0) - jnp.where(offset == -1, FIRST_COEF, 0.0) + jnp.where(offset == 2, SECOND_COEF, 0.0) - jnp.where(offset == -2, SECOND_COEF, 0.0)).astype(jnp.float32)
    below_diag = jnp.where(positions > 0, ALPHA_SIDE, 0.0).astype(jnp.float32)
    above_diag = jnp.where(positions < count - 1, ALPHA_SIDE, 0.0).astype(jnp.float32)
    middle = jnp.ones((count,), jnp.float32)
    return lax.linalg.tridiagonal_solve(below_diag, middle, above_diag, bmatrix)

def derive_rows(matrix, field):
    return jnp.einsum('ik,...kj->...ij', matrix, field, precision=lax.Precision.HIGHEST)

def derive_cols(matrix, field):
    return jnp.einsum('jk,...ik->...ij', matrix, field, precision=lax.Precision.HIGHEST)

def cross_three(first, second):
    return jnp.stack([first[1] * second[2] - first[2] * second[1], first[2] * second[0] - first[0] * second[2], first[0] * second[1] - first[1] * second[0]])

def flux_divergence(coords, flow, op_rows, op_cols):
    along_rows = derive_rows(op_rows, coords)
    along_cols = derive_cols(op_cols, coords)
    normal = cross_three(along_rows, along_cols)
    weight = 1.0 + jnp.sum(normal * normal, axis=0)
    flux_rows = jnp.sum(flow * cross_three(along_cols, normal), axis=0) / weight
    flux_cols = jnp.sum(flow * cross_three(normal, along_rows), axis=0) / weight
    return derive_rows(op_rows, flux_rows) + derive_cols(op_cols, flux_cols)

def reference(modal_blocks, amplitudes, owner_map, span_interp, chord_interp, base_coords, flow_state, face_rows, face_owner):
    op_rows = compact_operator(LI)
    op_cols = compact_operator(LJ)
    residuals = []
    fringes = []
    for blade_id in range(BLADES):
        root = owner_map[blade_id].astype(jnp.int32)
        blocks = lax.dynamic_slice_in_dim(modal_blocks[blade_id], (root * MODES).astype(jnp.int32), MODES, 0)
        shape_sum = jnp.sum(amplitudes[blade_id][:, None, None, None] * blocks, axis=0)
        spanwise = jnp.einsum('sr,cst->crt', span_interp[blade_id], shape_sum, precision=lax.Precision.HIGHEST)
        spanwise = spanwise.reshape(3, N_GRID, LI, SJ)
        chord = chord_interp[blade_id].reshape(N_GRID, SJ, LJ)
        displace = jnp.einsum('cgrt,gtj->cgrj', spanwise, chord, precision=lax.Precision.HIGHEST)
        coords = base_coords[blade_id].reshape(3, N_GRID, LI, LJ) + displace
        flow = flow_state[blade_id].reshape(3, N_GRID, LI, LJ)
        result = flux_divergence(coords, flow, op_rows, op_cols)
        residuals.append(result.reshape(N_GRID * LI, LJ))
        flat = coords.reshape(3, N_GRID * LI, LJ)
        donors = jnp.arange(N_GRID, dtype=jnp.int32)
        global_rows = (donors[:, None] * LI + face_rows[blade_id].reshape(N_GRID, NF)).reshape(-1)
        faces = jnp.transpose(flat[:, global_rows, :], (1, 0, 2))
        target = face_owner[blade_id, :, 0].reshape(N_GRID, NF)
        order = jnp.arange(NF)
        earlier = (target[:, :, None] == target[:, None, :]) & (order[None, None, :] < order[None, :, None])
        slot = jnp.sum(earlier.astype(jnp.int32), axis=2)
        place = (target * (N_GRID * CAP) + donors[:, None] * CAP + slot).reshape(-1).astype(jnp.int32)
        fringe = jnp.zeros((N_GRID * N_GRID * CAP, 3, LJ), jnp.float32).at[place].set(faces)
        fringes.append(fringe)
    return (jnp.stack(residuals), jnp.stack(fringes))
```

```python
import jax
import jax.numpy as jnp
import numpy as np
from jax import lax
from jax.sharding import PartitionSpec as P

CAP = 2


ALPHA_SIDE = 1.0 / 3.0
FIRST_COEF = 7.0 / 9.0
SECOND_COEF = 1.0 / 36.0


def spread(value, axis, source):
    kept = jnp.where(lax.axis_index(axis) == source, value, 0).astype(value.dtype)
    return lax.psum(kept, axis)


def compact_operator(count):
    positions = np.arange(count)
    offset = positions[None, :] - positions[:, None]
    bmatrix = (
        np.where(offset == 1, FIRST_COEF, 0.0)
        - np.where(offset == -1, FIRST_COEF, 0.0)
        + np.where(offset == 2, SECOND_COEF, 0.0)
        - np.where(offset == -2, SECOND_COEF, 0.0)
    )
    amatrix = np.eye(count) + np.where(np.abs(offset) == 1, ALPHA_SIDE, 0.0)
    return jnp.asarray(np.linalg.solve(amatrix, bmatrix).astype(np.float32))


def derive_rows(matrix, field):
    return jnp.einsum("ik,...kj->...ij", matrix, field, precision=lax.Precision.HIGHEST)


def derive_cols(matrix, field):
    return jnp.einsum("jk,...ik->...ij", matrix, field, precision=lax.Precision.HIGHEST)


def cross_three(first, second):
    return jnp.stack(
        [
            first[1] * second[2] - first[2] * second[1],
            first[2] * second[0] - first[0] * second[2],
            first[0] * second[1] - first[1] * second[0],
        ]
    )


def flux_divergence(coords, flow, op_rows, op_cols):
    along_rows = derive_rows(op_rows, coords)
    along_cols = derive_cols(op_cols, coords)
    normal = cross_three(along_rows, along_cols)
    weight = 1.0 + jnp.sum(normal * normal, axis=0)
    flux_rows = jnp.sum(flow * cross_three(along_cols, normal), axis=0) / weight
    flux_cols = jnp.sum(flow * cross_three(normal, along_rows), axis=0) / weight
    return derive_rows(op_rows, flux_rows) + derive_cols(op_cols, flux_cols)


def body(
    modal_blocks,
    amplitudes,
    owner_map,
    span_interp,
    chord_interp,
    base_coords,
    flow_state,
    face_rows,
    face_owner,
):
    local_sum = jnp.sum(amplitudes[0][:, None, None, None] * modal_blocks[0], axis=0)
    shape_sum = spread(local_sum, "grid", owner_map[0])
    spanwise = jnp.einsum("sr,cst->crt", span_interp[0], shape_sum, precision=lax.Precision.HIGHEST)
    displace = jnp.einsum("crt,tj->crj", spanwise, chord_interp[0], precision=lax.Precision.HIGHEST)
    coords = base_coords[0] + displace
    rows_local = coords.shape[1]
    width = coords.shape[2]
    peers = lax.axis_size("grid")
    count_faces = face_rows.shape[1]
    picker = (face_rows[0][:, None] == jnp.arange(rows_local, dtype=jnp.int32)[None, :]).astype(
        jnp.float32
    )
    faces = jnp.einsum("fi,cij->fcj", picker, coords, precision=lax.Precision.HIGHEST)
    target = face_owner[0, :, 0]
    order = jnp.arange(count_faces)
    earlier = (target[:, None] == target[None, :]) & (order[None, :] < order[:, None])
    slot = jnp.sum(earlier.astype(jnp.int32), axis=1)
    place = target * CAP + slot
    table = (place[None, :] == jnp.arange(peers * CAP, dtype=jnp.int32)[:, None]).astype(
        jnp.float32
    )
    outgoing = jnp.einsum("pf,fcj->pcj", table, faces, precision=lax.Precision.HIGHEST)
    outgoing = outgoing.reshape(peers, CAP, 3, width)
    arrived = lax.all_to_all(outgoing, "grid", split_axis=0, concat_axis=0, tiled=True)
    fringe = arrived.reshape(1, peers * CAP, 3, width)
    op_rows = compact_operator(rows_local)
    op_cols = compact_operator(width)
    result = flux_divergence(coords, flow_state[0], op_rows, op_cols)
    return (result[None], fringe)


def solution(mesh):
    return jax.shard_map(
        body,
        mesh=mesh,
        in_specs=(
            P("blade", "grid", None, None, None),
            P("blade", None),
            P("blade"),
            P("blade", None, "grid"),
            P("blade", "grid", None),
            P("blade", None, "grid", None),
            P("blade", None, "grid", None),
            P("blade", "grid"),
            P("blade", "grid", None),
        ),
        out_specs=(P("blade", "grid", None), P("blade", "grid", None, None)),
        check_vma=False,
    )
```

```python
import functools

import jax
import jax.numpy as jnp
import numpy as np
from jax import lax
from jax.experimental import pallas as pl
from jax.experimental.pallas import tpu as pltpu
from jax.sharding import PartitionSpec as P

ALPHA_SIDE = 1.0 / 3.0
FIRST_COEF = 7.0 / 9.0
SECOND_COEF = 1.0 / 36.0

MODES, SI, SJ = 24, 16, 128
LI, LJ = 32, 256
CAP, NF = 2, 96
NY, NZ, NX, NC = 8, 2, 4, 2
NP = NZ * NX * NC
MESH = pl.DeviceIdType.MESH
HIGHEST = lax.Precision.HIGHEST


def compact_operator(count):
    positions = np.arange(count)
    offset = positions[None, :] - positions[:, None]
    bmatrix = (
        np.where(offset == 1, FIRST_COEF, 0.0)
        - np.where(offset == -1, FIRST_COEF, 0.0)
        + np.where(offset == 2, SECOND_COEF, 0.0)
        - np.where(offset == -2, SECOND_COEF, 0.0)
    )
    amatrix = np.eye(count) + np.where(np.abs(offset) == 1, ALPHA_SIDE, 0.0)
    return np.linalg.solve(amatrix, bmatrix).astype(np.float32)


def dot(first, second):
    return jnp.dot(first, second, precision=HIGHEST, preferred_element_type=jnp.float32)


def cross_three(first, second):
    return [
        first[1] * second[2] - first[2] * second[1],
        first[2] * second[0] - first[0] * second[2],
        first[0] * second[1] - first[1] * second[0],
    ]


def dot_three(first, second):
    return first[0] * second[0] + first[1] * second[1] + first[2] * second[2]


def slot_table(rows, owner):
    faces = lax.broadcasted_iota(jnp.int32, (1, NF), 1)
    code = (faces * 64 + rows).astype(jnp.float32)
    both = jnp.concatenate([code, owner.astype(jnp.float32)], axis=0)
    both = jnp.concatenate([both, jnp.zeros((6, NF), jnp.float32)], axis=0)
    both = jnp.concatenate([both, jnp.zeros((8, 128 - NF), jnp.float32)], axis=1)
    cols = jnp.transpose(both)[:NF]
    code_col, owner_col = cols[:, 0:1], cols[:, 1:2]
    slots = lax.broadcasted_iota(jnp.int32, (NF, NY * NP * CAP), 1)
    hit = owner_col == (slots // CAP).astype(jnp.float32)
    big = 1.0e6
    first = jnp.min(jnp.where(hit, code_col, big), axis=0, keepdims=True)
    last = jnp.max(jnp.where(hit, code_col, -1.0), axis=0, keepdims=True)
    lane = lax.broadcasted_iota(jnp.int32, (1, NY * NP * CAP), 1)
    is_first = lane % CAP == 0
    pick = jnp.where(is_first, first, last)
    pick_row = pick - 64.0 * jnp.floor(pick * (1.0 / 64.0))
    margin = jnp.where(is_first, last + 1.0, last - first)
    return jnp.where(margin > 0.0, pick_row, float(LI))


def kernel(
    amp_ref,
    root_ref,
    modal_hbm,
    span_hbm,
    chord_hbm,
    base_hbm,
    flow_hbm,
    rows_ref,
    owner_ref,
    op_rows_ref,
    op_cols_hbm,
    result_ref,
    fringe_hbm,
    modal,
    span,
    chord,
    base,
    flow,
    op_cols,
    chunk_out,
    chunk_in,
    pick_out,
    pick_in,
    part_out,
    part_in,
    table_out,
    table_in,
    block,
    chosen,
    load_sem,
    phase_send,
    phase_recv,
    table_send,
    table_recv,
    ring_send,
    ring_recv,
    plane_send,
    plane_recv,
    self_sem,
):
    me = lax.axis_index("grid")
    my_y, my_p = me // NP, me % NP
    my_z, my_x, my_c = my_p // (NX * NC), (my_p // NC) % NX, my_p % NC

    def at_y(step):
        return lax.rem(my_y + step, NY)

    def device_y(step):
        return {"grid": at_y(step) * NP + my_p}

    offsets = [(dz, dx, dc) for dz in range(NZ) for dx in range(NX) for dc in range(NC)][1:]
    peers = [
        (lax.rem(my_z + dz, NZ) * NX + lax.rem(my_x + dx, NX)) * NC + lax.rem(my_c + dc, NC)
        for dz, dx, dc in offsets
    ]

    def device_p(peer):
        return {"grid": my_y * NP + peer}

    barrier = pltpu.get_barrier_semaphore()
    for peer in peers:
        pl.semaphore_signal(barrier, inc=1, device_id=device_p(peer), device_id_type=MESH)
    for step in range(1, NY):
        pl.semaphore_signal(barrier, inc=1, device_id=device_y(step), device_id_type=MESH)

    loads = [
        pltpu.make_async_copy(source, target, load_sem.at[number])
        for number, (source, target) in enumerate(
            [
                (modal_hbm, modal),
                (span_hbm, span),
                (chord_hbm, chord),
                (base_hbm, base),
                (flow_hbm, flow),
                (op_cols_hbm, op_cols),
            ]
        )
    ]
    for load in loads:
        load.start()

    table = slot_table(rows_ref[...], owner_ref[...])
    table_out[...] = table
    table_in[0] = table

    loads[0].wait()
    shape = amp_ref[0, 0] * modal[0]
    for mode in range(1, MODES):
        shape = shape + amp_ref[0, mode] * modal[mode]
    for s in range(SI):
        for comp in range(3):
            chunk_out[s, comp : comp + 1, :] = shape[comp, s : s + 1, :]
    chunk_in[my_p] = chunk_out[my_p]

    pl.semaphore_wait(barrier, len(peers) + NY - 1)

    root_y, root_p = root_ref[0] // NP, root_ref[0] % NP

    def exchange_plane(source_of, target, number):
        copies = [
            pltpu.make_async_remote_copy(
                src_ref=source_of(peer),
                dst_ref=target.at[my_p],
                send_sem=phase_send.at[number],
                recv_sem=phase_recv.at[number],
                device_id=device_p(peer),
                device_id_type=MESH,
            )
            for peer in peers
        ]
        for copy in copies:
            copy.start()

    def await_all(ref, send_sem, recv_sem):
        pltpu.make_async_copy(ref, ref, recv_sem).wait()
        pltpu.make_async_copy(ref, ref, send_sem).wait()

    exchange_plane(lambda peer: chunk_out.at[peer], chunk_in, 0)

    for step in range(1, NY):
        pltpu.make_async_remote_copy(
            src_ref=table_out,
            dst_ref=table_in.at[step],
            send_sem=table_send,
            recv_sem=table_recv,
            device_id=device_y(step),
            device_id_type=MESH,
        ).start()

    await_all(chunk_in.at[pl.ds(0, NP - 1)], phase_send.at[0], phase_recv.at[0])
    picked = chunk_in[root_p]
    pick_out[...] = picked
    pick_in[my_y] = picked
    for step in range(1, NY):
        pltpu.make_async_remote_copy(
            src_ref=pick_out,
            dst_ref=pick_in.at[my_y],
            send_sem=phase_send.at[1],
            recv_sem=phase_recv.at[1],
            device_id=device_y(step),
            device_id_type=MESH,
        ).start()
    await_all(pick_in.at[pl.ds(0, NY - 1)], phase_send.at[1], phase_recv.at[1])
    part = pick_in[root_y]
    part_out[...] = part
    part_in[my_p] = part
    exchange_plane(lambda peer: part_out, part_in, 2)

    await_all(table_in.at[pl.ds(0, NY - 1)], table_send, table_recv)
    tables = pltpu.roll(table_in[:, 0, :], lax.rem(NY - my_y, NY) * (NP * CAP), 1)
    table_cols = jnp.transpose(tables[:, :128])[: NP * CAP]

    for load in loads[1:]:
        load.wait()
    await_all(part_in.at[pl.ds(0, NP - 1)], phase_send.at[2], phase_recv.at[2])

    for comp in range(3):
        spanwise = lax.dot_general(
            span[...],
            part_in[:, comp, :],
            (((0,), (0,)), ((), ())),
            precision=HIGHEST,
            preferred_element_type=jnp.float32,
        )
        block[0, comp] = base[comp] + dot(spanwise, chord[...])

    def ring(index, comp, forward, half=False):
        later = lax.rem(index + (1 if forward else NY - 1), NY)
        source, target = block.at[index, comp], block.at[later, comp]
        if half:
            rows = pl.ds(0 if forward else LI // 2, LI // 2)
            source, target = source.at[rows], target.at[rows]
        way = 0 if forward else 1
        hop = later if forward else NY - later
        return pltpu.make_async_remote_copy(
            src_ref=source,
            dst_ref=target,
            send_sem=ring_send.at[way, hop - 1, comp],
            recv_sem=ring_recv.at[way, hop - 1, comp],
            device_id=device_y(1 if forward else NY - 1),
            device_id_type=MESH,
        )

    sent = []

    def send_ring(index, comp, forward, half=False):
        copy = ring(index, comp, forward, half)
        copy.start()
        sent.append(copy)

    def choose(index):
        lanes = lax.broadcasted_iota(jnp.int32, (NP * CAP, 3 * LI), 1) % LI
        hot = table_cols[:, index : index + 1] == lanes.astype(jnp.float32)
        hot = jnp.where(hot, 1.0, 0.0).astype(jnp.bfloat16)
        for comp in range(3):
            values = block[index, comp]
            high = values.astype(jnp.bfloat16)
            rest = values - high.astype(jnp.float32)
            middle = rest.astype(jnp.bfloat16)
            low = (rest - middle.astype(jnp.float32)).astype(jnp.bfloat16)
            stacked = jnp.concatenate([high, middle, low], axis=0)
            slots = jnp.dot(hot, stacked, preferred_element_type=jnp.float32)
            for peer in range(NP):
                chosen[index, peer, comp] = slots[CAP * peer : CAP * peer + CAP]
        donor = at_y(NY - index)
        for peer in peers:
            pltpu.make_async_remote_copy(
                src_ref=chosen.at[index, peer],
                dst_ref=fringe_hbm.at[donor, my_p],
                send_sem=plane_send,
                recv_sem=plane_recv,
                device_id=device_p(peer),
                device_id_type=MESH,
            ).start()
        copy = pltpu.make_async_copy(
            chosen.at[index, my_p], fringe_hbm.at[donor, my_p], self_sem.at[index]
        )
        copy.start()
        return copy

    for comp in range(3):
        send_ring(0, comp, True)
        send_ring(0, comp, False)
    own = [choose(0)]

    coords = [block[0, comp] for comp in range(3)]
    along_rows = [dot(op_rows_ref[...], coords[comp]) for comp in range(3)]
    along_cols = [dot(coords[comp], op_cols[...]) for comp in range(3)]
    normal = cross_three(along_rows, along_cols)
    weight = 1.0 + dot_three(normal, normal)
    stream = [flow[comp] for comp in range(3)]
    flux_rows = dot_three(stream, cross_three(along_cols, normal)) / weight
    flux_cols = dot_three(stream, cross_three(normal, along_rows)) / weight
    result_ref[...] = dot(op_rows_ref[...], flux_rows) + dot(flux_cols, op_cols[...])

    for hop in range(1, NY // 2 + 1):
        last = hop == NY // 2
        for comp in range(3):
            ring(hop - 1, comp, True, last).wait_recv()
            if not last:
                send_ring(hop, comp, True, hop == NY // 2 - 1)
            ring((NY - hop + 1) % NY, comp, False, last).wait_recv()
            if not last:
                send_ring(NY - hop, comp, False, hop == NY // 2 - 1)
        own.append(choose(hop))
        if not last:
            own.append(choose(NY - hop))

    for copy in sent:
        copy.wait_send()
    for copy in own:
        copy.wait()
    await_all(chosen.at[:, pl.ds(0, NP - 1)], plane_send, plane_recv)


def body(
    modal_blocks,
    amplitudes,
    owner_map,
    span_interp,
    chord_interp,
    base_coords,
    flow_state,
    face_rows,
    face_owner,
):
    op_rows = jnp.asarray(compact_operator(LI))
    op_cols = jnp.asarray(np.ascontiguousarray(compact_operator(LJ).T))
    vmem = pl.BlockSpec(memory_space=pltpu.VMEM)
    smem = pl.BlockSpec(memory_space=pltpu.SMEM)
    hbm = pl.BlockSpec(memory_space=pl.ANY)
    f32 = jnp.float32
    result, fringe = pl.pallas_call(
        kernel,
        out_shape=(
            jax.ShapeDtypeStruct((LI, LJ), f32),
            jax.ShapeDtypeStruct((NY, NP, 3, CAP, LJ), f32),
        ),
        in_specs=[smem, smem, hbm, hbm, hbm, hbm, hbm, vmem, vmem, vmem, hbm],
        out_specs=(vmem, hbm),
        scratch_shapes=[
            pltpu.VMEM((MODES, 3, SI, SJ), f32),
            pltpu.VMEM((SI, LI), f32),
            pltpu.VMEM((SJ, LJ), f32),
            pltpu.VMEM((3, LI, LJ), f32),
            pltpu.VMEM((3, LI, LJ), f32),
            pltpu.VMEM((LJ, LJ), f32),
            pltpu.VMEM((NP, 3, SJ), f32),
            pltpu.VMEM((NP, 3, SJ), f32),
            pltpu.VMEM((3, SJ), f32),
            pltpu.VMEM((NY, 3, SJ), f32),
            pltpu.VMEM((3, SJ), f32),
            pltpu.VMEM((NP, 3, SJ), f32),
            pltpu.VMEM((1, NY * NP * CAP), f32),
            pltpu.VMEM((NY, 1, NY * NP * CAP), f32),
            pltpu.VMEM((NY, 3, LI, LJ), f32),
            pltpu.VMEM((NY, NP, 3, CAP, LJ), f32),
            pltpu.SemaphoreType.DMA((6,)),
            pltpu.SemaphoreType.DMA((3,)),
            pltpu.SemaphoreType.DMA((3,)),
            pltpu.SemaphoreType.DMA,
            pltpu.SemaphoreType.DMA,
            pltpu.SemaphoreType.DMA((2, 4, 3)),
            pltpu.SemaphoreType.DMA((2, 4, 3)),
            pltpu.SemaphoreType.DMA,
            pltpu.SemaphoreType.DMA,
            pltpu.SemaphoreType.DMA((NY,)),
        ],
        compiler_params=pltpu.CompilerParams(collective_id=0, has_side_effects=True),
        name="section",
    )(
        amplitudes,
        owner_map,
        modal_blocks[0],
        span_interp[0],
        chord_interp[0],
        base_coords[0],
        flow_state[0],
        face_rows,
        face_owner.reshape(1, NF),
        op_rows,
        op_cols,
    )
    fringe = fringe.reshape(NY * NP, 3, CAP, LJ).transpose(0, 2, 1, 3)
    return (result[None], fringe.reshape(1, NY * NP * CAP, 3, LJ))


def solution(mesh):
    return jax.shard_map(
        body,
        mesh=mesh,
        in_specs=(
            P("blade", "grid", None, None, None),
            P("blade", None),
            P("blade"),
            P("blade", None, "grid"),
            P("blade", "grid", None),
            P("blade", None, "grid", None),
            P("blade", None, "grid", None),
            P("blade", "grid"),
            P("blade", "grid", None),
        ),
        out_specs=(P("blade", "grid", None), P("blade", "grid", None, None)),
        check_vma=False,
    )
```

```python
import jax
import jax.numpy as jnp
import numpy as np
from jax import lax
from jax.experimental import pallas as pl
from jax.experimental.pallas import tpu as pltpu
from jax.sharding import PartitionSpec as P

ALPHA_SIDE = 1.0 / 3.0
FIRST_COEF = 7.0 / 9.0
SECOND_COEF = 1.0 / 36.0

MODES, SI, SJ = 24, 16, 128
LI, LJ = 32, 256
CAP, NF = 2, 96
NY, NZ, NX, NC = 8, 2, 4, 2
NP = NZ * NX * NC
MESH = pl.DeviceIdType.MESH
HIGHEST = lax.Precision.HIGHEST


def compact_operator(count):
    positions = np.arange(count)
    offset = positions[None, :] - positions[:, None]
    bmatrix = (
        np.where(offset == 1, FIRST_COEF, 0.0)
        - np.where(offset == -1, FIRST_COEF, 0.0)
        + np.where(offset == 2, SECOND_COEF, 0.0)
        - np.where(offset == -2, SECOND_COEF, 0.0)
    )
    amatrix = np.eye(count) + np.where(np.abs(offset) == 1, ALPHA_SIDE, 0.0)
    return np.linalg.solve(amatrix, bmatrix).astype(np.float32)


def dot(first, second):
    return jnp.dot(first, second, precision=HIGHEST, preferred_element_type=jnp.float32)


def cross_three(first, second):
    return [
        first[1] * second[2] - first[2] * second[1],
        first[2] * second[0] - first[0] * second[2],
        first[0] * second[1] - first[1] * second[0],
    ]


def dot_three(first, second):
    return first[0] * second[0] + first[1] * second[1] + first[2] * second[2]


def slot_table(rows, owner):
    faces = lax.broadcasted_iota(jnp.int32, (1, NF), 1)
    code = (faces * 64 + rows).astype(jnp.float32)
    both = jnp.concatenate([code, owner.astype(jnp.float32)], axis=0)
    both = jnp.concatenate([both, jnp.zeros((6, NF), jnp.float32)], axis=0)
    both = jnp.concatenate([both, jnp.zeros((8, 128 - NF), jnp.float32)], axis=1)
    cols = jnp.transpose(both)[:NF]
    code_col, owner_col = cols[:, 0:1], cols[:, 1:2]
    slots = lax.broadcasted_iota(jnp.int32, (NF, NY * NP * CAP), 1)
    hit = owner_col == (slots // CAP).astype(jnp.float32)
    big = 1.0e6
    first = jnp.min(jnp.where(hit, code_col, big), axis=0, keepdims=True)
    last = jnp.max(jnp.where(hit, code_col, -1.0), axis=0, keepdims=True)
    lane = lax.broadcasted_iota(jnp.int32, (1, NY * NP * CAP), 1)
    is_first = lane % CAP == 0
    pick = jnp.where(is_first, first, last)
    pick_row = pick - 64.0 * jnp.floor(pick * (1.0 / 64.0))
    margin = jnp.where(is_first, last + 1.0, last - first)
    return jnp.where(margin > 0.0, pick_row, float(LI))


def kernel(
    root_hbm,
    amp_hbm,
    rows_hbm,
    owner_hbm,
    modal_hbm,
    span_hbm,
    chord_hbm,
    base_hbm,
    flow_hbm,
    op_rows_hbm,
    op_cols_hbm,
    result_hbm,
    fringe_hbm,
    root_ref,
    amp_ref,
    rows_ref,
    owner_ref,
    modal,
    span,
    chord,
    base,
    flow,
    op_rows_ref,
    op_cols,
    result,
    local_sum,
    core_in,
    chip_in,
    plane_in,
    shape_in,
    table_out,
    table_in,
    block,
    chosen,
    load_sem,
    phase_send,
    phase_recv,
    table_send,
    table_recv,
    ring_send,
    ring_recv,
    plane_send,
    plane_recv,
    self_sem,
    result_sem,
):
    me = lax.axis_index("grid")
    my_y, my_p = me // NP, me % NP
    my_q, my_c = my_p // NC, my_p % NC
    my_z, my_x = my_q // NX, my_q % NX

    def at_y(step):
        return lax.rem(my_y + step, NY)

    def device_y(step):
        return {"grid": at_y(step) * NP + my_p}

    def peer_at(dz, dx, dc):
        z, x, c = lax.rem(my_z + dz, NZ), lax.rem(my_x + dx, NX), lax.rem(my_c + dc, NC)
        return (z * NX + x) * NC + c

    def device_p(peer):
        return {"grid": my_y * NP + peer}

    far_first = [(dz, dx) for dz in (1, 0) for dx in (2, 1, 3, 0)]
    peers = [peer_at(dz, dx, dc) for dc in (1, 0) for dz, dx in far_first][:-1]
    chips = [peer_at(dz, dx, 0) for dz, dx in far_first][:-1]
    partner = peer_at(0, 0, 1)
    y_steps = (4, 3, 5, 2, 6, 1, 7)

    loads = [
        pltpu.make_async_copy(source, target, load_sem.at[number])
        for number, (source, target) in enumerate(
            [
                (modal_hbm, modal),
                (root_hbm, root_ref),
                (amp_hbm, amp_ref),
                (rows_hbm, rows_ref),
                (owner_hbm, owner_ref),
                (span_hbm, span),
                (chord_hbm, chord),
                (base_hbm, base),
                (flow_hbm, flow),
                (op_rows_hbm, op_rows_ref),
                (op_cols_hbm, op_cols),
            ]
        )
    ]
    for load in loads[:5]:
        load.start()

    barrier = pltpu.get_barrier_semaphore()
    for step in y_steps:
        pl.semaphore_signal(barrier, inc=1, device_id=device_y(step), device_id_type=MESH)
    for peer in peers:
        pl.semaphore_signal(barrier, inc=1, device_id=device_p(peer), device_id_type=MESH)

    for load in loads[1:5]:
        load.wait()
    table = slot_table(rows_ref[...], owner_ref[...])
    table_out[...] = table
    table_in[0] = table

    loads[0].wait()
    for load in loads[5:]:
        load.start()
    shape = amp_ref[0, 0] * modal[0]
    for mode in range(1, MODES):
        shape = shape + amp_ref[0, mode] * modal[mode]
    shape = shape.reshape(3 * SI, SJ)
    half_rows = 3 * SI // NC
    for half in range(NC):
        local_sum[half] = shape[half * half_rows : (half + 1) * half_rows]
    core_in[my_c] = local_sum[my_c]

    pl.semaphore_wait(barrier, len(peers) + len(y_steps))

    root = root_ref[0]
    root_y, root_q, root_c = root // NP, (root % NP) // NC, root % NC

    def send(source, target, number, device):
        pltpu.make_async_remote_copy(
            src_ref=source,
            dst_ref=target,
            send_sem=phase_send.at[number],
            recv_sem=phase_recv.at[number],
            device_id=device,
            device_id_type=MESH,
        ).start()

    def await_all(ref, send_sem, recv_sem):
        pltpu.make_async_copy(ref, ref, recv_sem).wait()
        pltpu.make_async_copy(ref, ref, send_sem).wait()

    send(local_sum.at[1 - my_c], core_in.at[my_c], 0, device_p(partner))
    await_all(core_in.at[0], phase_send.at[0], phase_recv.at[0])
    chip_in[my_q] = core_in[root_c]
    for peer in chips:
        send(chip_in.at[my_q], chip_in.at[my_q], 1, device_p(peer))
    for step in y_steps:
        pltpu.make_async_remote_copy(
            src_ref=table_out,
            dst_ref=table_in.at[step],
            send_sem=table_send,
            recv_sem=table_recv,
            device_id=device_y(step),
            device_id_type=MESH,
        ).start()
    await_all(chip_in.at[pl.ds(0, NP // NC - 1)], phase_send.at[1], phase_recv.at[1])
    plane_in[my_y] = chip_in[root_q]
    for step in y_steps:
        send(plane_in.at[my_y], plane_in.at[my_y], 2, device_y(step))

    await_all(table_in.at[pl.ds(0, NY - 1)], table_send, table_recv)
    tables = pltpu.roll(table_in[:, 0, :], lax.rem(NY - my_y, NY) * (NP * CAP), 1)
    table_cols = jnp.transpose(tables[:, :128])[: NP * CAP]
    for load in loads[5:]:
        load.wait()

    await_all(plane_in.at[pl.ds(0, NY - 1)], phase_send.at[2], phase_recv.at[2])
    shape_in[my_c] = plane_in[root_y]
    send(shape_in.at[my_c], shape_in.at[my_c], 3, device_p(partner))
    await_all(shape_in.at[0], phase_send.at[3], phase_recv.at[3])
    shape_sum = shape_in[...].reshape(3 * SI, SJ)

    def ring(index, comp, half, forward, step=1):
        later = (index + (step if forward else NY - step)) % NY
        rows = pl.ds(half * (LI // 2), LI // 2)
        way = 0 if forward else 1
        hop = later if forward else NY - later
        return pltpu.make_async_remote_copy(
            src_ref=block.at[index, comp, rows],
            dst_ref=block.at[later, comp, rows],
            send_sem=ring_send.at[way, hop - 1, comp * 2 + half],
            recv_sem=ring_recv.at[way, hop - 1, comp * 2 + half],
            device_id=device_y(step if forward else NY - step),
            device_id_type=MESH,
        )

    sent = []

    def send_ring(index, comp, half, forward, step=1):
        copy = ring(index, comp, half, forward, step)
        copy.start()
        sent.append(copy)

    def hot_rows(index):
        lanes = lax.broadcasted_iota(jnp.int32, (NP * CAP, 3 * LI), 1) % LI
        hot = table_cols[:, index : index + 1] == lanes.astype(jnp.float32)
        return jnp.where(hot, 1.0, 0.0).astype(jnp.bfloat16)

    own = []

    def slots_of(donor):
        return pl.ds(pl.multiple_of((donor * NP + my_p) * CAP, CAP), CAP)

    def choose(index, comp, hot):
        values = block[index, comp]
        high = values.astype(jnp.bfloat16)
        rest = values - high.astype(jnp.float32)
        middle = rest.astype(jnp.bfloat16)
        low = (rest - middle.astype(jnp.float32)).astype(jnp.bfloat16)
        stacked = jnp.concatenate([high, middle, low], axis=0)
        slots = jnp.dot(hot, stacked, preferred_element_type=jnp.float32)
        for peer in range(NP):
            chosen[index, comp, peer] = slots[CAP * peer : CAP * peer + CAP]
        place = slots_of(at_y(NY - index))
        single = index in (3, 4, 5)
        if comp < 2 and not single:
            return
        comps = comp if single else slice(None)
        for peer in peers:
            pltpu.make_async_remote_copy(
                src_ref=chosen.at[index, comps, peer],
                dst_ref=fringe_hbm.at[comps, place],
                send_sem=plane_send,
                recv_sem=plane_recv,
                device_id=device_p(peer),
                device_id_type=MESH,
            ).start()
        if comp == 2:
            copy = pltpu.make_async_copy(
                chosen.at[index, :, my_p], fringe_hbm.at[:, place], self_sem.at[index]
            )
            copy.start()
            own.append(copy)

    for comp in range(3):
        spanwise = lax.dot_general(
            span[...],
            shape_sum[comp * SI : (comp + 1) * SI],
            (((0,), (0,)), ((), ())),
            precision=HIGHEST,
            preferred_element_type=jnp.float32,
        )
        block[0, comp] = base[comp] + dot(spanwise, chord[...])
        for half in range(2):
            send_ring(0, comp, half, True)
            send_ring(0, comp, half, False)
    hot = hot_rows(0)
    for comp in range(3):
        choose(0, comp, hot)

    coords = [block[0, comp] for comp in range(3)]
    along_rows = [dot(op_rows_ref[...], coords[comp]) for comp in range(3)]
    along_cols = [dot(coords[comp], op_cols[...]) for comp in range(3)]
    normal = cross_three(along_rows, along_cols)
    weight = 1.0 + dot_three(normal, normal)
    stream = [flow[comp] for comp in range(3)]
    flux_rows = dot_three(stream, cross_three(along_cols, normal)) / weight
    flux_cols = dot_three(stream, cross_three(normal, along_rows)) / weight
    result[...] = dot(op_rows_ref[...], flux_rows) + dot(flux_cols, op_cols[...])
    leave = pltpu.make_async_copy(result, result_hbm, result_sem)
    leave.start()

    for hop in range(1, NY // 2 + 1):
        last = hop == NY // 2
        hot_up, hot_down = hot_rows(hop), hot_rows(NY - hop)
        for comp in range(3):
            for half in range(2):
                if last:
                    ring(2 if half == 0 else NY - 2, comp, half, half == 0, 2).wait_recv()
                    continue
                ring(hop - 1, comp, half, True).wait_recv()
                if hop < 3:
                    send_ring(hop, comp, half, True)
                if hop == 2 and half == 0:
                    send_ring(hop, comp, half, True, 2)
                ring((NY - hop + 1) % NY, comp, half, False).wait_recv()
                if hop < 3:
                    send_ring(NY - hop, comp, half, False)
                if hop == 2 and half == 1:
                    send_ring(NY - hop, comp, half, False, 2)
            choose(hop, comp, hot_up)
            if not last:
                choose(NY - hop, comp, hot_down)

    for copy in sent:
        copy.wait_send()
    for copy in own:
        copy.wait()
    leave.wait()
    await_all(chosen.at[:, :, pl.ds(0, NP - 1)], plane_send, plane_recv)


def body(
    modal_blocks,
    amplitudes,
    owner_map,
    span_interp,
    chord_interp,
    base_coords,
    flow_state,
    face_rows,
    face_owner,
):
    op_rows = jnp.asarray(compact_operator(LI))
    op_cols = jnp.asarray(np.ascontiguousarray(compact_operator(LJ).T))
    hbm = pl.BlockSpec(memory_space=pltpu.HBM)
    free = pl.BlockSpec(memory_space=pl.ANY)
    f32 = jnp.float32
    result, fringe = pl.pallas_call(
        kernel,
        out_shape=(
            jax.ShapeDtypeStruct((LI, LJ), f32),
            jax.ShapeDtypeStruct((3, NY * NP * CAP, LJ), f32),
        ),
        in_specs=[free] + [hbm] * 10,
        out_specs=(free, free),
        scratch_shapes=[
            pltpu.SMEM((1,), jnp.int32),
            pltpu.SMEM((1, MODES), f32),
            pltpu.VMEM((1, NF), jnp.int32),
            pltpu.VMEM((1, NF), jnp.int32),
            pltpu.VMEM((MODES, 3, SI, SJ), f32),
            pltpu.VMEM((SI, LI), f32),
            pltpu.VMEM((SJ, LJ), f32),
            pltpu.VMEM((3, LI, LJ), f32),
            pltpu.VMEM((3, LI, LJ), f32),
            pltpu.VMEM((LI, LI), f32),
            pltpu.VMEM((LJ, LJ), f32),
            pltpu.VMEM((LI, LJ), f32),
            pltpu.VMEM((NC, 3 * SI // NC, SJ), f32),
            pltpu.VMEM((NC, 3 * SI // NC, SJ), f32),
            pltpu.VMEM((NP // NC, 3 * SI // NC, SJ), f32),
            pltpu.VMEM((NY, 3 * SI // NC, SJ), f32),
            pltpu.VMEM((NC, 3 * SI // NC, SJ), f32),
            pltpu.VMEM((1, NY * NP * CAP), f32),
            pltpu.VMEM((NY, 1, NY * NP * CAP), f32),
            pltpu.VMEM((NY, 3, LI, LJ), f32),
            pltpu.VMEM((NY, 3, NP, CAP, LJ), f32),
            pltpu.SemaphoreType.DMA((11,)),
            pltpu.SemaphoreType.DMA((4,)),
            pltpu.SemaphoreType.DMA((4,)),
            pltpu.SemaphoreType.DMA,
            pltpu.SemaphoreType.DMA,
            pltpu.SemaphoreType.DMA((2, 4, 6)),
            pltpu.SemaphoreType.DMA((2, 4, 6)),
            pltpu.SemaphoreType.DMA,
            pltpu.SemaphoreType.DMA,
            pltpu.SemaphoreType.DMA((NY,)),
            pltpu.SemaphoreType.DMA,
        ],
        compiler_params=pltpu.CompilerParams(collective_id=0, has_side_effects=True, vmem_limit_bytes=12 << 20),
        name="section",
    )(
        owner_map,
        *(
            pltpu.with_memory_space_constraint(array, pltpu.HBM)
            for array in (
                amplitudes,
                face_rows,
                face_owner.reshape(1, NF),
                modal_blocks[0],
                span_interp[0],
                chord_interp[0],
                base_coords[0],
                flow_state[0],
                op_rows,
                op_cols,
            )
        ),
    )
    return (result[None], fringe.transpose(1, 0, 2)[None])


def solution(mesh):
    return jax.shard_map(
        body,
        mesh=mesh,
        in_specs=(
            P("blade", "grid", None, None, None),
            P("blade", None),
            P("blade"),
            P("blade", None, "grid"),
            P("blade", "grid", None),
            P("blade", None, "grid", None),
            P("blade", None, "grid", None),
            P("blade", "grid"),
            P("blade", "grid", None),
        ),
        out_specs=(P("blade", "grid", None), P("blade", "grid", None, None)),
        check_vma=False,
    )
```

```python
import jax
import jax.numpy as jnp
import numpy as np
from jax import lax
from jax.experimental import pallas as pl
from jax.experimental.pallas import tpu as pltpu
from jax.sharding import PartitionSpec as P

ALPHA_SIDE = 1.0 / 3.0
FIRST_COEF = 7.0 / 9.0
SECOND_COEF = 1.0 / 36.0

MODES, SI, SJ = 24, 16, 128
LI, LJ = 32, 256
CAP, NF = 2, 96
NY, NZ, NX, NC = 8, 2, 4, 2
NP = NZ * NX * NC
MESH = pl.DeviceIdType.MESH
HIGHEST = lax.Precision.HIGHEST


def compact_operator(count):
    positions = np.arange(count)
    offset = positions[None, :] - positions[:, None]
    bmatrix = (
        np.where(offset == 1, FIRST_COEF, 0.0)
        - np.where(offset == -1, FIRST_COEF, 0.0)
        + np.where(offset == 2, SECOND_COEF, 0.0)
        - np.where(offset == -2, SECOND_COEF, 0.0)
    )
    amatrix = np.eye(count) + np.where(np.abs(offset) == 1, ALPHA_SIDE, 0.0)
    return np.linalg.solve(amatrix, bmatrix).astype(np.float32)


def dot(first, second):
    return jnp.dot(first, second, precision=HIGHEST, preferred_element_type=jnp.float32)


def cross_three(first, second):
    return [
        first[1] * second[2] - first[2] * second[1],
        first[2] * second[0] - first[0] * second[2],
        first[0] * second[1] - first[1] * second[0],
    ]


def dot_three(first, second):
    return first[0] * second[0] + first[1] * second[1] + first[2] * second[2]


def slot_table(rows, owner):
    faces = lax.broadcasted_iota(jnp.int32, (1, NF), 1)
    code = (faces * 64 + rows).astype(jnp.float32)
    both = jnp.concatenate([code, owner.astype(jnp.float32)], axis=0)
    both = jnp.concatenate([both, jnp.zeros((6, NF), jnp.float32)], axis=0)
    both = jnp.concatenate([both, jnp.zeros((8, 128 - NF), jnp.float32)], axis=1)
    cols = jnp.transpose(both)[:NF]
    code_col, owner_col = cols[:, 0:1], cols[:, 1:2]
    slots = lax.broadcasted_iota(jnp.int32, (NF, NY * NP * CAP), 1)
    hit = owner_col == (slots // CAP).astype(jnp.float32)
    big = 1.0e6
    first = jnp.min(jnp.where(hit, code_col, big), axis=0, keepdims=True)
    last = jnp.max(jnp.where(hit, code_col, -1.0), axis=0, keepdims=True)
    lane = lax.broadcasted_iota(jnp.int32, (1, NY * NP * CAP), 1)
    is_first = lane % CAP == 0
    pick = jnp.where(is_first, first, last)
    pick_row = pick - 64.0 * jnp.floor(pick * (1.0 / 64.0))
    margin = jnp.where(is_first, last + 1.0, last - first)
    return jnp.where(margin > 0.0, pick_row, float(LI))


def kernel(
    root_hbm,
    amp_hbm,
    rows_hbm,
    owner_hbm,
    modal_hbm,
    span_hbm,
    chord_hbm,
    base_hbm,
    flow_hbm,
    op_rows_hbm,
    op_cols_hbm,
    result_hbm,
    fringe_hbm,
    root_ref,
    amp_ref,
    rows_ref,
    owner_ref,
    modal,
    span,
    chord,
    base,
    flow,
    op_rows_ref,
    op_cols,
    near_span,
    near_chord,
    near_base,
    result,
    local_sum,
    core_in,
    chip_in,
    plane_in,
    shape_in,
    table_out,
    table_in,
    block,
    chosen,
    load_sem,
    phase_send,
    phase_recv,
    table_send,
    table_recv,
    ring_send,
    ring_recv,
    plane_send,
    plane_recv,
    self_sem,
    result_sem,
    near_send,
    near_recv,
):
    me = lax.axis_index("grid")
    my_y, my_p = me // NP, me % NP
    my_q, my_c = my_p // NC, my_p % NC
    my_z, my_x = my_q // NX, my_q % NX

    def at_y(step):
        return lax.rem(my_y + step, NY)

    def device_y(step):
        return {"grid": at_y(step) * NP + my_p}

    def peer_at(dz, dx, dc):
        z, x, c = lax.rem(my_z + dz, NZ), lax.rem(my_x + dx, NX), lax.rem(my_c + dc, NC)
        return (z * NX + x) * NC + c

    def device_p(peer):
        return {"grid": my_y * NP + peer}

    far_first = [(dz, dx) for dz in (1, 0) for dx in (2, 1, 3, 0)]
    peers = [peer_at(dz, dx, dc) for dc in (1, 0) for dz, dx in far_first][:-1]
    chips = [peer_at(dz, dx, 0) for dz, dx in far_first][:-1]
    partner = peer_at(0, 0, 1)
    y_steps = (4, 3, 5, 2, 6, 1, 7)

    loads = [
        pltpu.make_async_copy(source, target, load_sem.at[number])
        for number, (source, target) in enumerate(
            [
                (modal_hbm, modal),
                (root_hbm, root_ref),
                (amp_hbm, amp_ref),
                (rows_hbm, rows_ref),
                (owner_hbm, owner_ref),
                (span_hbm, span),
                (chord_hbm, chord),
                (base_hbm, base),
                (flow_hbm, flow),
                (op_rows_hbm, op_rows_ref),
                (op_cols_hbm, op_cols),
            ]
        )
    ]
    for load in loads[:5]:
        load.start()

    barrier = pltpu.get_barrier_semaphore()
    for step in y_steps:
        pl.semaphore_signal(barrier, inc=1, device_id=device_y(step), device_id_type=MESH)
    for peer in peers:
        pl.semaphore_signal(barrier, inc=1, device_id=device_p(peer), device_id_type=MESH)

    for load in loads[1:5]:
        load.wait()
    table = slot_table(rows_ref[...], owner_ref[...])
    table_out[...] = table
    table_in[0] = table

    loads[0].wait()
    for load in loads[5:]:
        load.start()
    shape = amp_ref[0, 0] * modal[0]
    for mode in range(1, MODES):
        shape = shape + amp_ref[0, mode] * modal[mode]
    shape = shape.reshape(3 * SI, SJ)
    half_rows = 3 * SI // NC
    for half in range(NC):
        local_sum[half] = shape[half * half_rows : (half + 1) * half_rows]
    core_in[my_c] = local_sum[my_c]

    pl.semaphore_wait(barrier, len(peers) + len(y_steps))

    root = root_ref[0]
    root_y, root_q, root_c = root // NP, (root % NP) // NC, root % NC

    def send(source, target, number, device):
        pltpu.make_async_remote_copy(
            src_ref=source,
            dst_ref=target,
            send_sem=phase_send.at[number],
            recv_sem=phase_recv.at[number],
            device_id=device,
            device_id_type=MESH,
        ).start()

    def await_all(ref, send_sem, recv_sem):
        pltpu.make_async_copy(ref, ref, recv_sem).wait()
        pltpu.make_async_copy(ref, ref, send_sem).wait()

    send(local_sum.at[1 - my_c], core_in.at[my_c], 0, device_p(partner))
    near = [
        pltpu.make_async_remote_copy(
            src_ref=source,
            dst_ref=target.at[way],
            send_sem=near_send.at[way, number],
            recv_sem=near_recv.at[way, number],
            device_id=device_y(1 if way == 0 else NY - 1),
            device_id_type=MESH,
        )
        for number, (source, target) in enumerate(
            [(span_hbm, near_span), (chord_hbm, near_chord), (base_hbm, near_base)]
        )
        for way in range(2)
    ]
    for copy in near:
        copy.start()
    await_all(core_in.at[0], phase_send.at[0], phase_recv.at[0])
    chip_in[my_q] = core_in[root_c]
    for peer in chips:
        send(chip_in.at[my_q], chip_in.at[my_q], 1, device_p(peer))
    for step in y_steps:
        pltpu.make_async_remote_copy(
            src_ref=table_out,
            dst_ref=table_in.at[step],
            send_sem=table_send,
            recv_sem=table_recv,
            device_id=device_y(step),
            device_id_type=MESH,
        ).start()
    await_all(chip_in.at[pl.ds(0, NP // NC - 1)], phase_send.at[1], phase_recv.at[1])
    plane_in[my_y] = chip_in[root_q]
    for step in y_steps:
        send(plane_in.at[my_y], plane_in.at[my_y], 2, device_y(step))

    await_all(table_in.at[pl.ds(0, NY - 1)], table_send, table_recv)
    tables = pltpu.roll(table_in[:, 0, :], lax.rem(NY - my_y, NY) * (NP * CAP), 1)
    table_cols = jnp.transpose(tables[:, :128])[: NP * CAP]
    for load in loads[5:]:
        load.wait()

    await_all(plane_in.at[pl.ds(0, NY - 1)], phase_send.at[2], phase_recv.at[2])
    shape_in[my_c] = plane_in[root_y]
    send(shape_in.at[my_c], shape_in.at[my_c], 3, device_p(partner))
    for copy in near:
        copy.wait()
    await_all(shape_in.at[0], phase_send.at[3], phase_recv.at[3])
    shape_sum = shape_in[...].reshape(3 * SI, SJ)

    def ring(index, comp, half, forward, step=1):
        later = (index + (step if forward else NY - step)) % NY
        rows = pl.ds(half * (LI // 2), LI // 2)
        way = 0 if forward else 1
        hop = later if forward else NY - later
        return pltpu.make_async_remote_copy(
            src_ref=block.at[index, comp, rows],
            dst_ref=block.at[later, comp, rows],
            send_sem=ring_send.at[way, hop - 1, comp * 2 + half],
            recv_sem=ring_recv.at[way, hop - 1, comp * 2 + half],
            device_id=device_y(step if forward else NY - step),
            device_id_type=MESH,
        )

    sent = []

    def send_ring(index, comp, half, forward, step=1):
        copy = ring(index, comp, half, forward, step)
        copy.start()
        sent.append(copy)

    def hot_rows(index):
        lanes = lax.broadcasted_iota(jnp.int32, (NP * CAP, 3 * LI), 1) % LI
        hot = table_cols[:, index : index + 1] == lanes.astype(jnp.float32)
        return jnp.where(hot, 1.0, 0.0).astype(jnp.bfloat16)

    own = []

    def slots_of(donor):
        return pl.ds(pl.multiple_of((donor * NP + my_p) * CAP, CAP), CAP)

    def choose(index, comp, hot):
        values = block[index, comp]
        high = values.astype(jnp.bfloat16)
        rest = values - high.astype(jnp.float32)
        middle = rest.astype(jnp.bfloat16)
        low = (rest - middle.astype(jnp.float32)).astype(jnp.bfloat16)
        stacked = jnp.concatenate([high, middle, low], axis=0)
        slots = jnp.dot(hot, stacked, preferred_element_type=jnp.float32)
        for peer in range(NP):
            chosen[index, comp, peer] = slots[CAP * peer : CAP * peer + CAP]
        place = slots_of(at_y(NY - index))
        single = index in (3, 4, 5)
        if comp < 2 and not single:
            return
        comps = comp if single else slice(None)
        for peer in peers:
            pltpu.make_async_remote_copy(
                src_ref=chosen.at[index, comps, peer],
                dst_ref=fringe_hbm.at[comps, place],
                send_sem=plane_send,
                recv_sem=plane_recv,
                device_id=device_p(peer),
                device_id_type=MESH,
            ).start()
        if comp == 2:
            copy = pltpu.make_async_copy(
                chosen.at[index, :, my_p], fringe_hbm.at[:, place], self_sem.at[index]
            )
            copy.start()
            own.append(copy)

    def displaced(index, span_of, chord_of, base_of):
        spanwise = [
            lax.dot_general(
                span_of[...],
                shape_sum[comp * SI : (comp + 1) * SI],
                (((0,), (0,)), ((), ())),
                precision=HIGHEST,
                preferred_element_type=jnp.float32,
            )
            for comp in range(3)
        ]
        moved = dot(jnp.concatenate(spanwise, axis=0), chord_of[...])
        for comp in range(3):
            block[index, comp] = base_of[comp] + moved[comp * LI : (comp + 1) * LI]

    for way, index in ((0, 1), (1, NY - 1)):
        displaced(index, near_span.at[way], near_chord.at[way], near_base.at[way])
        for comp in range(3):
            for half in range(2):
                send_ring(index, comp, half, way == 0)
    displaced(0, span, chord, base)
    for index in (1, NY - 1, 0):
        hot = hot_rows(index)
        for comp in range(3):
            choose(index, comp, hot)

    coords = [block[0, comp] for comp in range(3)]
    along_rows = [dot(op_rows_ref[...], coords[comp]) for comp in range(3)]
    along_cols = [dot(coords[comp], op_cols[...]) for comp in range(3)]
    normal = cross_three(along_rows, along_cols)
    weight = 1.0 + dot_three(normal, normal)
    stream = [flow[comp] for comp in range(3)]
    flux_rows = dot_three(stream, cross_three(along_cols, normal)) / weight
    flux_cols = dot_three(stream, cross_three(normal, along_rows)) / weight
    result[...] = dot(op_rows_ref[...], flux_rows) + dot(flux_cols, op_cols[...])
    leave = pltpu.make_async_copy(result, result_hbm, result_sem)
    leave.start()

    for hop in range(2, NY // 2 + 1):
        last = hop == NY // 2
        hot_up, hot_down = hot_rows(hop), hot_rows(NY - hop)
        for comp in range(3):
            for half in range(2):
                if last:
                    ring(2 if half == 0 else NY - 2, comp, half, half == 0, 2).wait_recv()
                    continue
                ring(hop - 1, comp, half, True).wait_recv()
                if hop < 3:
                    send_ring(hop, comp, half, True)
                if hop == 2 and half == 0:
                    send_ring(hop, comp, half, True, 2)
                ring((NY - hop + 1) % NY, comp, half, False).wait_recv()
                if hop < 3:
                    send_ring(NY - hop, comp, half, False)
                if hop == 2 and half == 1:
                    send_ring(NY - hop, comp, half, False, 2)
            choose(hop, comp, hot_up)
            if not last:
                choose(NY - hop, comp, hot_down)

    for copy in sent:
        copy.wait_send()
    for copy in own:
        copy.wait()
    leave.wait()
    await_all(chosen.at[:, :, pl.ds(0, NP - 1)], plane_send, plane_recv)


def body(
    modal_blocks,
    amplitudes,
    owner_map,
    span_interp,
    chord_interp,
    base_coords,
    flow_state,
    face_rows,
    face_owner,
):
    op_rows = jnp.asarray(compact_operator(LI))
    op_cols = jnp.asarray(np.ascontiguousarray(compact_operator(LJ).T))
    hbm = pl.BlockSpec(memory_space=pltpu.HBM)
    free = pl.BlockSpec(memory_space=pl.ANY)
    f32 = jnp.float32
    result, fringe = pl.pallas_call(
        kernel,
        out_shape=(
            jax.ShapeDtypeStruct((LI, LJ), f32),
            jax.ShapeDtypeStruct((3, NY * NP * CAP, LJ), f32),
        ),
        in_specs=[free] + [hbm] * 10,
        out_specs=(free, free),
        scratch_shapes=[
            pltpu.SMEM((1,), jnp.int32),
            pltpu.SMEM((1, MODES), f32),
            pltpu.VMEM((1, NF), jnp.int32),
            pltpu.VMEM((1, NF), jnp.int32),
            pltpu.VMEM((MODES, 3, SI, SJ), f32),
            pltpu.VMEM((SI, LI), f32),
            pltpu.VMEM((SJ, LJ), f32),
            pltpu.VMEM((3, LI, LJ), f32),
            pltpu.VMEM((3, LI, LJ), f32),
            pltpu.VMEM((LI, LI), f32),
            pltpu.VMEM((LJ, LJ), f32),
            pltpu.VMEM((2, SI, LI), f32),
            pltpu.VMEM((2, SJ, LJ), f32),
            pltpu.VMEM((2, 3, LI, LJ), f32),
            pltpu.VMEM((LI, LJ), f32),
            pltpu.VMEM((NC, 3 * SI // NC, SJ), f32),
            pltpu.VMEM((NC, 3 * SI // NC, SJ), f32),
            pltpu.VMEM((NP // NC, 3 * SI // NC, SJ), f32),
            pltpu.VMEM((NY, 3 * SI // NC, SJ), f32),
            pltpu.VMEM((NC, 3 * SI // NC, SJ), f32),
            pltpu.VMEM((1, NY * NP * CAP), f32),
            pltpu.VMEM((NY, 1, NY * NP * CAP), f32),
            pltpu.VMEM((NY, 3, LI, LJ), f32),
            pltpu.VMEM((NY, 3, NP, CAP, LJ), f32),
            pltpu.SemaphoreType.DMA((11,)),
            pltpu.SemaphoreType.DMA((4,)),
            pltpu.SemaphoreType.DMA((4,)),
            pltpu.SemaphoreType.DMA,
            pltpu.SemaphoreType.DMA,
            pltpu.SemaphoreType.DMA((2, 4, 6)),
            pltpu.SemaphoreType.DMA((2, 4, 6)),
            pltpu.SemaphoreType.DMA,
            pltpu.SemaphoreType.DMA,
            pltpu.SemaphoreType.DMA((NY,)),
            pltpu.SemaphoreType.DMA,
            pltpu.SemaphoreType.DMA((2, 3)),
            pltpu.SemaphoreType.DMA((2, 3)),
        ],
        compiler_params=pltpu.CompilerParams(collective_id=0, has_side_effects=True, vmem_limit_bytes=12 << 20),
        name="section",
    )(
        owner_map,
        *(
            pltpu.with_memory_space_constraint(array, pltpu.HBM)
            for array in (
                amplitudes,
                face_rows,
                face_owner.reshape(1, NF),
                modal_blocks[0],
                span_interp[0],
                chord_interp[0],
                base_coords[0],
                flow_state[0],
                op_rows,
                op_cols,
            )
        ),
    )
    return (result[None], fringe.transpose(1, 0, 2)[None])


def solution(mesh):
    return jax.shard_map(
        body,
        mesh=mesh,
        in_specs=(
            P("blade", "grid", None, None, None),
            P("blade", None),
            P("blade"),
            P("blade", None, "grid"),
            P("blade", "grid", None),
            P("blade", None, "grid", None),
            P("blade", None, "grid", None),
            P("blade", "grid"),
            P("blade", "grid", None),
        ),
        out_specs=(P("blade", "grid", None), P("blade", "grid", None, None)),
        check_vma=False,
    )
```

```python
import jax
import jax.numpy as jnp
import numpy as np
from jax import lax
from jax.experimental import pallas as pl
from jax.experimental.pallas import tpu as pltpu
from jax.sharding import PartitionSpec as P

ALPHA_SIDE = 1.0 / 3.0
FIRST_COEF = 7.0 / 9.0
SECOND_COEF = 1.0 / 36.0

MODES, SI, SJ = 24, 16, 128
LI, LJ = 32, 256
CAP, NF = 2, 96
NY, NZ, NX, NC = 8, 2, 4, 2
NP = NZ * NX * NC
MESH = pl.DeviceIdType.MESH
HIGHEST = lax.Precision.HIGHEST


def compact_operator(count):
    positions = np.arange(count)
    offset = positions[None, :] - positions[:, None]
    bmatrix = (
        np.where(offset == 1, FIRST_COEF, 0.0)
        - np.where(offset == -1, FIRST_COEF, 0.0)
        + np.where(offset == 2, SECOND_COEF, 0.0)
        - np.where(offset == -2, SECOND_COEF, 0.0)
    )
    amatrix = np.eye(count) + np.where(np.abs(offset) == 1, ALPHA_SIDE, 0.0)
    return np.linalg.solve(amatrix, bmatrix).astype(np.float32)


def dot(first, second):
    return jnp.dot(first, second, precision=HIGHEST, preferred_element_type=jnp.float32)


def split(values):
    high = values.astype(jnp.bfloat16)
    return high, (values - high.astype(jnp.float32)).astype(jnp.bfloat16)


def cross_three(first, second):
    return [
        first[1] * second[2] - first[2] * second[1],
        first[2] * second[0] - first[0] * second[2],
        first[0] * second[1] - first[1] * second[0],
    ]


def dot_three(first, second):
    return first[0] * second[0] + first[1] * second[1] + first[2] * second[2]


def slot_table(rows, owner):
    faces = lax.broadcasted_iota(jnp.int32, (1, NF), 1)
    code = (faces * 64 + rows).astype(jnp.float32)
    both = jnp.concatenate([code, owner.astype(jnp.float32)], axis=0)
    both = jnp.concatenate([both, jnp.zeros((6, NF), jnp.float32)], axis=0)
    both = jnp.concatenate([both, jnp.zeros((8, 128 - NF), jnp.float32)], axis=1)
    cols = jnp.transpose(both)[:NF]
    code_col, owner_col = cols[:, 0:1], cols[:, 1:2]
    slots = lax.broadcasted_iota(jnp.int32, (NF, NY * NP * CAP), 1)
    hit = owner_col == (slots // CAP).astype(jnp.float32)
    big = 1.0e6
    first = jnp.min(jnp.where(hit, code_col, big), axis=0, keepdims=True)
    last = jnp.max(jnp.where(hit, code_col, -1.0), axis=0, keepdims=True)
    lane = lax.broadcasted_iota(jnp.int32, (1, NY * NP * CAP), 1)
    is_first = lane % CAP == 0
    pick = jnp.where(is_first, first, last)
    pick_row = pick - 64.0 * jnp.floor(pick * (1.0 / 64.0))
    margin = jnp.where(is_first, last + 1.0, last - first)
    return jnp.where(margin > 0.0, pick_row, float(LI))


def kernel(
    root_hbm,
    amp_hbm,
    rows_hbm,
    owner_hbm,
    modal_hbm,
    span_hbm,
    chord_hbm,
    base_hbm,
    flow_hbm,
    op_rows_hbm,
    op_cols_hbm,
    result_hbm,
    fringe_hbm,
    root_ref,
    amp_ref,
    rows_ref,
    owner_ref,
    modal,
    span,
    chord,
    base,
    flow,
    op_rows_ref,
    op_cols,
    near_span,
    near_chord,
    near_base,
    span_parts,
    chord_parts,
    result,
    local_sum,
    core_in,
    chip_in,
    plane_in,
    shape_in,
    table_out,
    table_in,
    block,
    chosen,
    load_sem,
    phase_send,
    phase_recv,
    table_send,
    table_recv,
    ring_send,
    ring_recv,
    plane_send,
    plane_recv,
    self_sem,
    result_sem,
    near_send,
    near_recv,
):
    me = lax.axis_index("grid")
    my_y, my_p = me // NP, me % NP
    my_q, my_c = my_p // NC, my_p % NC
    my_z, my_x = my_q // NX, my_q % NX

    def at_y(step):
        return lax.rem(my_y + step, NY)

    def device_y(step):
        return {"grid": at_y(step) * NP + my_p}

    def peer_at(dz, dx, dc):
        z, x, c = lax.rem(my_z + dz, NZ), lax.rem(my_x + dx, NX), lax.rem(my_c + dc, NC)
        return (z * NX + x) * NC + c

    def device_p(peer):
        return {"grid": my_y * NP + peer}

    far_first = [(dz, dx) for dz in (1, 0) for dx in (2, 1, 3, 0)]
    peers = [peer_at(dz, dx, dc) for dc in (1, 0) for dz, dx in far_first][:-1]
    chips = [peer_at(dz, dx, 0) for dz, dx in far_first][:-1]
    partner = peer_at(0, 0, 1)
    y_steps = (4, 3, 5, 2, 6, 1, 7)

    loads = [
        pltpu.make_async_copy(source, target, load_sem.at[number])
        for number, (source, target) in enumerate(
            [
                (modal_hbm, modal),
                (root_hbm, root_ref),
                (amp_hbm, amp_ref),
                (rows_hbm, rows_ref),
                (owner_hbm, owner_ref),
                (span_hbm, span),
                (chord_hbm, chord),
                (base_hbm, base),
                (flow_hbm, flow),
                (op_rows_hbm, op_rows_ref),
                (op_cols_hbm, op_cols),
            ]
        )
    ]
    for load in loads[:5]:
        load.start()

    barrier = pltpu.get_barrier_semaphore()
    for step in y_steps:
        pl.semaphore_signal(barrier, inc=1, device_id=device_y(step), device_id_type=MESH)
    for peer in peers:
        pl.semaphore_signal(barrier, inc=1, device_id=device_p(peer), device_id_type=MESH)

    for load in loads[1:5]:
        load.wait()
    table = slot_table(rows_ref[...], owner_ref[...])
    table_out[...] = table
    table_in[0] = table

    loads[0].wait()
    for load in loads[5:]:
        load.start()
    shape = amp_ref[0, 0] * modal[0]
    for mode in range(1, MODES):
        shape = shape + amp_ref[0, mode] * modal[mode]
    shape = shape.reshape(3 * SI, SJ)
    half_rows = 3 * SI // NC
    for half in range(NC):
        local_sum[half] = shape[half * half_rows : (half + 1) * half_rows]
    core_in[my_c] = local_sum[my_c]

    pl.semaphore_wait(barrier, len(peers) + len(y_steps))

    root = root_ref[0]
    root_y, root_q, root_c = root // NP, (root % NP) // NC, root % NC

    def send(source, target, number, device):
        pltpu.make_async_remote_copy(
            src_ref=source,
            dst_ref=target,
            send_sem=phase_send.at[number],
            recv_sem=phase_recv.at[number],
            device_id=device,
            device_id_type=MESH,
        ).start()

    def await_all(ref, send_sem, recv_sem):
        pltpu.make_async_copy(ref, ref, recv_sem).wait()
        pltpu.make_async_copy(ref, ref, send_sem).wait()

    send(local_sum.at[1 - my_c], core_in.at[my_c], 0, device_p(partner))
    near = [
        pltpu.make_async_remote_copy(
            src_ref=source,
            dst_ref=target.at[way],
            send_sem=near_send.at[way, number],
            recv_sem=near_recv.at[way, number],
            device_id=device_y(1 if way == 0 else NY - 1),
            device_id_type=MESH,
        )
        for number, (source, target) in enumerate(
            [(span, near_span), (chord, near_chord), (base, near_base)]
        )
        for way in range(2)
    ]
    for load in loads[5:8]:
        load.wait()
    for copy in near:
        copy.start()
    await_all(core_in.at[0], phase_send.at[0], phase_recv.at[0])
    chip_in[my_q] = core_in[root_c]
    for peer in chips:
        send(chip_in.at[my_q], chip_in.at[my_q], 1, device_p(peer))
    for step in y_steps:
        pltpu.make_async_remote_copy(
            src_ref=table_out,
            dst_ref=table_in.at[step],
            send_sem=table_send,
            recv_sem=table_recv,
            device_id=device_y(step),
            device_id_type=MESH,
        ).start()
    await_all(chip_in.at[pl.ds(0, NP // NC - 1)], phase_send.at[1], phase_recv.at[1])
    plane_in[my_y] = chip_in[root_q]
    for step in y_steps:
        send(plane_in.at[my_y], plane_in.at[my_y], 2, device_y(step))

    await_all(table_in.at[pl.ds(0, NY - 1)], table_send, table_recv)
    tables = pltpu.roll(table_in[:, 0, :], lax.rem(NY - my_y, NY) * (NP * CAP), 1)
    table_cols = jnp.transpose(tables[:, :128])[: NP * CAP]
    for load in loads[8:]:
        load.wait()

    await_all(plane_in.at[pl.ds(0, NY - 1)], phase_send.at[2], phase_recv.at[2])
    shape_in[my_c] = plane_in[root_y]
    send(shape_in.at[my_c], shape_in.at[my_c], 3, device_p(partner))
    for copy in near:
        copy.wait()
    for number, (span_of, chord_of) in enumerate(
        [(near_span.at[0], near_chord.at[0]), (near_span.at[1], near_chord.at[1]), (span, chord)]
    ):
        high, low = split(span_of[...])
        span_parts[number] = jnp.concatenate([high, high, low], axis=0)
        high, low = split(chord_of[...])
        chord_parts[number] = jnp.concatenate([high, low, high], axis=0)
    await_all(shape_in.at[0], phase_send.at[3], phase_recv.at[3])
    shape_sum = shape_in[...].reshape(3 * SI, SJ)

    def ring(index, comp, half, forward, step=1):
        later = (index + (step if forward else NY - step)) % NY
        rows = pl.ds(half * (LI // 2), LI // 2)
        way = 0 if forward else 1
        hop = later if forward else NY - later
        return pltpu.make_async_remote_copy(
            src_ref=block.at[index, comp, rows],
            dst_ref=block.at[later, comp, rows],
            send_sem=ring_send.at[way, hop - 1, comp * 2 + half],
            recv_sem=ring_recv.at[way, hop - 1, comp * 2 + half],
            device_id=device_y(step if forward else NY - step),
            device_id_type=MESH,
        )

    sent = []

    def send_ring(index, comp, half, forward, step=1):
        copy = ring(index, comp, half, forward, step)
        copy.start()
        sent.append(copy)

    def hot_rows(index):
        lanes = lax.broadcasted_iota(jnp.int32, (NP * CAP, 3 * LI), 1) % LI
        hot = table_cols[:, index : index + 1] == lanes.astype(jnp.float32)
        return jnp.where(hot, 1.0, 0.0).astype(jnp.bfloat16)

    own = []

    def slots_of(donor):
        return pl.ds(pl.multiple_of((donor * NP + my_p) * CAP, CAP), CAP)

    def choose(index, comp, hot):
        values = block[index, comp]
        high = values.astype(jnp.bfloat16)
        rest = values - high.astype(jnp.float32)
        middle = rest.astype(jnp.bfloat16)
        low = (rest - middle.astype(jnp.float32)).astype(jnp.bfloat16)
        stacked = jnp.concatenate([high, middle, low], axis=0)
        slots = jnp.dot(hot, stacked, preferred_element_type=jnp.float32)
        for peer in range(NP):
            chosen[index, comp, peer] = slots[CAP * peer : CAP * peer + CAP]
        place = slots_of(at_y(NY - index))
        single = index in (3, 4, 5)
        if comp < 2 and not single:
            return
        comps = comp if single else slice(None)
        for peer in peers:
            pltpu.make_async_remote_copy(
                src_ref=chosen.at[index, comps, peer],
                dst_ref=fringe_hbm.at[comps, place],
                send_sem=plane_send,
                recv_sem=plane_recv,
                device_id=device_p(peer),
                device_id_type=MESH,
            ).start()
        if comp == 2:
            copy = pltpu.make_async_copy(
                chosen.at[index, :, my_p], fringe_hbm.at[:, place], self_sem.at[index]
            )
            copy.start()
            own.append(copy)

    parts = [split(shape_sum[comp * SI : (comp + 1) * SI]) for comp in range(3)]
    wide_high = jnp.concatenate([high for high, _ in parts], axis=1)
    wide_low = jnp.concatenate([low for _, low in parts], axis=1)
    wide = jnp.concatenate([wide_high, wide_low, wide_high], axis=0)

    def displaced(index, number, base_of):
        spanwise = lax.dot_general(
            span_parts[number],
            wide,
            (((0,), (0,)), ((), ())),
            preferred_element_type=jnp.float32,
        )
        stacked = jnp.concatenate(
            [spanwise[:, comp * SJ : (comp + 1) * SJ] for comp in range(3)], axis=0
        )
        high, low = split(stacked)
        moved = jnp.dot(
            jnp.concatenate([high, high, low], axis=1),
            chord_parts[number],
            preferred_element_type=jnp.float32,
        )
        for comp in range(3):
            block[index, comp] = base_of[comp] + moved[comp * LI : (comp + 1) * LI]

    for way, index in ((0, 1), (1, NY - 1)):
        displaced(index, way, near_base.at[way])
        for comp in range(3):
            for half in range(2):
                send_ring(index, comp, half, way == 0)
    displaced(0, 2, base)
    for index in (1, NY - 1, 0):
        hot = hot_rows(index)
        for comp in range(3):
            choose(index, comp, hot)

    coords = [block[0, comp] for comp in range(3)]
    along_rows = [dot(op_rows_ref[...], coords[comp]) for comp in range(3)]
    along_cols = [dot(coords[comp], op_cols[...]) for comp in range(3)]
    normal = cross_three(along_rows, along_cols)
    weight = 1.0 + dot_three(normal, normal)
    stream = [flow[comp] for comp in range(3)]
    flux_rows = dot_three(stream, cross_three(along_cols, normal)) / weight
    flux_cols = dot_three(stream, cross_three(normal, along_rows)) / weight
    result[...] = dot(op_rows_ref[...], flux_rows) + dot(flux_cols, op_cols[...])
    leave = pltpu.make_async_copy(result, result_hbm, result_sem)
    leave.start()

    for hop in range(2, NY // 2 + 1):
        last = hop == NY // 2
        hot_up, hot_down = hot_rows(hop), hot_rows(NY - hop)
        for comp in range(3):
            for half in range(2):
                if last:
                    ring(2 if half == 0 else NY - 2, comp, half, half == 0, 2).wait_recv()
                    continue
                ring(hop - 1, comp, half, True).wait_recv()
                if hop < 3:
                    send_ring(hop, comp, half, True)
                if hop == 2 and half == 0:
                    send_ring(hop, comp, half, True, 2)
                ring((NY - hop + 1) % NY, comp, half, False).wait_recv()
                if hop < 3:
                    send_ring(NY - hop, comp, half, False)
                if hop == 2 and half == 1:
                    send_ring(NY - hop, comp, half, False, 2)
            choose(hop, comp, hot_up)
            if not last:
                choose(NY - hop, comp, hot_down)

    for copy in sent:
        copy.wait_send()
    for copy in own:
        copy.wait()
    leave.wait()
    await_all(chosen.at[:, :, pl.ds(0, NP - 1)], plane_send, plane_recv)


def leave(result_in, fringe_in, result_out, fringe_out, sem):
    copies = [
        pltpu.make_async_copy(result_in, result_out, sem.at[0]),
        pltpu.make_async_copy(fringe_in, fringe_out, sem.at[1]),
    ]
    for copy in copies:
        copy.start()
    for copy in copies:
        copy.wait()


def body(
    modal_blocks,
    amplitudes,
    owner_map,
    span_interp,
    chord_interp,
    base_coords,
    flow_state,
    face_rows,
    face_owner,
):
    op_rows = jnp.asarray(compact_operator(LI))
    op_cols = jnp.asarray(np.ascontiguousarray(compact_operator(LJ).T))
    hbm = pl.BlockSpec(memory_space=pltpu.HBM)
    free = pl.BlockSpec(memory_space=pl.ANY)
    f32 = jnp.float32
    result, fringe = pl.pallas_call(
        kernel,
        out_shape=(
            jax.ShapeDtypeStruct((LI, LJ), f32),
            jax.ShapeDtypeStruct((3, NY * NP * CAP, LJ), f32),
        ),
        in_specs=[free] + [hbm] * 10,
        out_specs=(free, free),
        scratch_shapes=[
            pltpu.SMEM((1,), jnp.int32),
            pltpu.SMEM((1, MODES), f32),
            pltpu.VMEM((1, NF), jnp.int32),
            pltpu.VMEM((1, NF), jnp.int32),
            pltpu.VMEM((MODES, 3, SI, SJ), f32),
            pltpu.VMEM((SI, LI), f32),
            pltpu.VMEM((SJ, LJ), f32),
            pltpu.VMEM((3, LI, LJ), f32),
            pltpu.VMEM((3, LI, LJ), f32),
            pltpu.VMEM((LI, LI), f32),
            pltpu.VMEM((LJ, LJ), f32),
            pltpu.VMEM((2, SI, LI), f32),
            pltpu.VMEM((2, SJ, LJ), f32),
            pltpu.VMEM((2, 3, LI, LJ), f32),
            pltpu.VMEM((3, 3 * SI, LI), jnp.bfloat16),
            pltpu.VMEM((3, 3 * SJ, LJ), jnp.bfloat16),
            pltpu.VMEM((LI, LJ), f32),
            pltpu.VMEM((NC, 3 * SI // NC, SJ), f32),
            pltpu.VMEM((NC, 3 * SI // NC, SJ), f32),
            pltpu.VMEM((NP // NC, 3 * SI // NC, SJ), f32),
            pltpu.VMEM((NY, 3 * SI // NC, SJ), f32),
            pltpu.VMEM((NC, 3 * SI // NC, SJ), f32),
            pltpu.VMEM((1, NY * NP * CAP), f32),
            pltpu.VMEM((NY, 1, NY * NP * CAP), f32),
            pltpu.VMEM((NY, 3, LI, LJ), f32),
            pltpu.VMEM((NY, 3, NP, CAP, LJ), f32),
            pltpu.SemaphoreType.DMA((11,)),
            pltpu.SemaphoreType.DMA((4,)),
            pltpu.SemaphoreType.DMA((4,)),
            pltpu.SemaphoreType.DMA,
            pltpu.SemaphoreType.DMA,
            pltpu.SemaphoreType.DMA((2, 4, 6)),
            pltpu.SemaphoreType.DMA((2, 4, 6)),
            pltpu.SemaphoreType.DMA,
            pltpu.SemaphoreType.DMA,
            pltpu.SemaphoreType.DMA((NY,)),
            pltpu.SemaphoreType.DMA,
            pltpu.SemaphoreType.DMA((2, 3)),
            pltpu.SemaphoreType.DMA((2, 3)),
        ],
        compiler_params=pltpu.CompilerParams(collective_id=0, has_side_effects=True, vmem_limit_bytes=12 << 20),
        name="section",
    )(
        owner_map,
        *(
            pltpu.with_memory_space_constraint(array, pltpu.HBM)
            for array in (
                amplitudes,
                face_rows,
                face_owner.reshape(1, NF),
                modal_blocks[0],
                span_interp[0],
                chord_interp[0],
                base_coords[0],
                flow_state[0],
                op_rows,
                op_cols,
            )
        ),
    )
    result, fringe = pl.pallas_call(
        leave,
        out_shape=(
            jax.ShapeDtypeStruct(result.shape, f32),
            jax.ShapeDtypeStruct(fringe.shape, f32),
        ),
        in_specs=[free, free],
        out_specs=(hbm, hbm),
        scratch_shapes=[pltpu.SemaphoreType.DMA((2,))],
        compiler_params=pltpu.CompilerParams(vmem_limit_bytes=1 << 20),
        name="leave",
    )(result, fringe)
    return (result[None], fringe.transpose(1, 0, 2)[None])


def solution(mesh):
    return jax.shard_map(
        body,
        mesh=mesh,
        in_specs=(
            P("blade", "grid", None, None, None),
            P("blade", None),
            P("blade"),
            P("blade", None, "grid"),
            P("blade", "grid", None),
            P("blade", None, "grid", None),
            P("blade", None, "grid", None),
            P("blade", "grid"),
            P("blade", "grid", None),
        ),
        out_specs=(P("blade", "grid", None), P("blade", "grid", None, None)),
        check_vma=False,
    )
```

```python
import jax
import jax.numpy as jnp
import numpy as np
from jax import lax
from jax.experimental import pallas as pl
from jax.experimental.pallas import tpu as pltpu
from jax.sharding import PartitionSpec as P

ALPHA_SIDE = 1.0 / 3.0
FIRST_COEF = 7.0 / 9.0
SECOND_COEF = 1.0 / 36.0

MODES, SI, SJ = 24, 16, 128
LI, LJ = 32, 256
CAP, NF = 2, 96
NY, NZ, NX, NC = 8, 2, 4, 2
NP = NZ * NX * NC
MESH = pl.DeviceIdType.MESH
HIGHEST = lax.Precision.HIGHEST


def compact_operator(count):
    positions = np.arange(count)
    offset = positions[None, :] - positions[:, None]
    bmatrix = (
        np.where(offset == 1, FIRST_COEF, 0.0)
        - np.where(offset == -1, FIRST_COEF, 0.0)
        + np.where(offset == 2, SECOND_COEF, 0.0)
        - np.where(offset == -2, SECOND_COEF, 0.0)
    )
    amatrix = np.eye(count) + np.where(np.abs(offset) == 1, ALPHA_SIDE, 0.0)
    return np.linalg.solve(amatrix, bmatrix).astype(np.float32)


def dot(first, second):
    return jnp.dot(first, second, precision=HIGHEST, preferred_element_type=jnp.float32)


def split(values):
    high = values.astype(jnp.bfloat16)
    return high, (values - high.astype(jnp.float32)).astype(jnp.bfloat16)


def cross_three(first, second):
    return [
        first[1] * second[2] - first[2] * second[1],
        first[2] * second[0] - first[0] * second[2],
        first[0] * second[1] - first[1] * second[0],
    ]


def dot_three(first, second):
    return first[0] * second[0] + first[1] * second[1] + first[2] * second[2]


def slot_table(rows, owner):
    faces = lax.broadcasted_iota(jnp.int32, (1, NF), 1)
    code = (faces * 64 + rows).astype(jnp.float32)
    both = jnp.concatenate([code, owner.astype(jnp.float32)], axis=0)
    both = jnp.concatenate([both, jnp.zeros((6, NF), jnp.float32)], axis=0)
    both = jnp.concatenate([both, jnp.zeros((8, 128 - NF), jnp.float32)], axis=1)
    cols = jnp.transpose(both)[:NF]
    code_col, owner_col = cols[:, 0:1], cols[:, 1:2]
    slots = lax.broadcasted_iota(jnp.int32, (NF, NY * NP * CAP), 1)
    hit = owner_col == (slots // CAP).astype(jnp.float32)
    big = 1.0e6
    first = jnp.min(jnp.where(hit, code_col, big), axis=0, keepdims=True)
    last = jnp.max(jnp.where(hit, code_col, -1.0), axis=0, keepdims=True)
    lane = lax.broadcasted_iota(jnp.int32, (1, NY * NP * CAP), 1)
    is_first = lane % CAP == 0
    pick = jnp.where(is_first, first, last)
    pick_row = pick - 64.0 * jnp.floor(pick * (1.0 / 64.0))
    margin = jnp.where(is_first, last + 1.0, last - first)
    return jnp.where(margin > 0.0, pick_row, float(LI))


def kernel(
    root_hbm,
    amp_hbm,
    rows_hbm,
    owner_hbm,
    modal_hbm,
    span_hbm,
    chord_hbm,
    base_hbm,
    flow_hbm,
    op_rows_hbm,
    op_cols_hbm,
    result_hbm,
    fringe_hbm,
    root_ref,
    amp_ref,
    rows_ref,
    owner_ref,
    modal,
    span,
    chord,
    base,
    flow,
    op_rows_ref,
    op_cols,
    near_span,
    near_chord,
    near_base,
    span_parts,
    chord_parts,
    result,
    local_sum,
    core_in,
    chip_in,
    plane_in,
    shape_in,
    table_out,
    table_in,
    block,
    chosen,
    load_sem,
    phase_send,
    phase_recv,
    table_send,
    table_recv,
    ring_send,
    ring_recv,
    plane_send,
    plane_recv,
    self_sem,
    result_sem,
    near_send,
    near_recv,
):
    me = lax.axis_index("grid")
    my_y, my_p = me // NP, me % NP
    my_q, my_c = my_p // NC, my_p % NC
    my_z, my_x = my_q // NX, my_q % NX

    def at_y(step):
        return lax.rem(my_y + step, NY)

    def device_y(step):
        return {"grid": at_y(step) * NP + my_p}

    def peer_at(dz, dx, dc):
        z, x, c = lax.rem(my_z + dz, NZ), lax.rem(my_x + dx, NX), lax.rem(my_c + dc, NC)
        return (z * NX + x) * NC + c

    def device_p(peer):
        return {"grid": my_y * NP + peer}

    far_first = [(dz, dx) for dz in (1, 0) for dx in (2, 1, 3, 0)]
    peers = [peer_at(dz, dx, dc) for dc in (1, 0) for dz, dx in far_first][:-1]
    chips = [peer_at(dz, dx, 0) for dz, dx in far_first][:-1]
    partner = peer_at(0, 0, 1)
    y_steps = (4, 3, 5, 2, 6, 1, 7)

    loads = [
        pltpu.make_async_copy(source, target, load_sem.at[number])
        for number, (source, target) in enumerate(
            [
                (modal_hbm, modal),
                (root_hbm, root_ref),
                (amp_hbm, amp_ref),
                (rows_hbm, rows_ref),
                (owner_hbm, owner_ref),
                (span_hbm, span),
                (chord_hbm, chord),
                (base_hbm, base),
                (flow_hbm, flow),
                (op_rows_hbm, op_rows_ref),
                (op_cols_hbm, op_cols),
            ]
        )
    ]
    for load in loads[:5]:
        load.start()

    barrier = pltpu.get_barrier_semaphore()
    for step in y_steps:
        pl.semaphore_signal(barrier, inc=1, device_id=device_y(step), device_id_type=MESH)
    for peer in peers:
        pl.semaphore_signal(barrier, inc=1, device_id=device_p(peer), device_id_type=MESH)

    for load in loads[1:5]:
        load.wait()
    table = slot_table(rows_ref[...], owner_ref[...])
    table_out[...] = table
    table_in[0] = table

    loads[0].wait()
    for load in loads[5:]:
        load.start()
    shape = amp_ref[0, 0] * modal[0]
    for mode in range(1, MODES):
        shape = shape + amp_ref[0, mode] * modal[mode]
    shape = shape.reshape(3 * SI, SJ)
    half_rows = 3 * SI // NC
    for half in range(NC):
        local_sum[half] = shape[half * half_rows : (half + 1) * half_rows]
    core_in[my_c] = local_sum[my_c]

    pl.semaphore_wait(barrier, len(peers) + len(y_steps))

    root = root_ref[0]
    root_y, root_q, root_c = root // NP, (root % NP) // NC, root % NC

    def send(source, target, number, device):
        pltpu.make_async_remote_copy(
            src_ref=source,
            dst_ref=target,
            send_sem=phase_send.at[number],
            recv_sem=phase_recv.at[number],
            device_id=device,
            device_id_type=MESH,
        ).start()

    def await_all(ref, send_sem, recv_sem):
        pltpu.make_async_copy(ref, ref, recv_sem).wait()
        pltpu.make_async_copy(ref, ref, send_sem).wait()

    send(local_sum.at[1 - my_c], core_in.at[my_c], 0, device_p(partner))
    near = [
        pltpu.make_async_remote_copy(
            src_ref=source,
            dst_ref=target.at[way],
            send_sem=near_send.at[way, number],
            recv_sem=near_recv.at[way, number],
            device_id=device_y(1 if way == 0 else NY - 1),
            device_id_type=MESH,
        )
        for number, (source, target) in enumerate(
            [(span, near_span), (chord, near_chord), (base, near_base)]
        )
        for way in range(2)
    ]
    for load in loads[5:8]:
        load.wait()
    for copy in near[:4]:
        copy.start()
    await_all(core_in.at[0], phase_send.at[0], phase_recv.at[0])
    chip_in[my_q] = core_in[root_c]
    for peer in chips:
        send(chip_in.at[my_q], chip_in.at[my_q], 1, device_p(peer))
    for step in y_steps:
        pltpu.make_async_remote_copy(
            src_ref=table_out,
            dst_ref=table_in.at[step],
            send_sem=table_send,
            recv_sem=table_recv,
            device_id=device_y(step),
            device_id_type=MESH,
        ).start()
    await_all(chip_in.at[pl.ds(0, NP // NC - 1)], phase_send.at[1], phase_recv.at[1])
    plane_in[my_y] = chip_in[root_q]
    for step in y_steps:
        send(plane_in.at[my_y], plane_in.at[my_y], 2, device_y(step))
    for copy in near[4:]:
        copy.start()

    await_all(table_in.at[pl.ds(0, NY - 1)], table_send, table_recv)
    tables = pltpu.roll(table_in[:, 0, :], lax.rem(NY - my_y, NY) * (NP * CAP), 1)
    table_cols = jnp.transpose(tables[:, :128])[: NP * CAP]
    for load in loads[8:]:
        load.wait()

    def split_parts(number, span_of, chord_of):
        high, low = split(span_of[...])
        span_parts[number] = jnp.concatenate([high, high, low], axis=0)
        high, low = split(chord_of[...])
        chord_parts[number] = jnp.concatenate([high, low, high], axis=0)

    split_parts(2, span, chord)
    await_all(plane_in.at[pl.ds(0, NY - 1)], phase_send.at[2], phase_recv.at[2])
    shape_in[my_c] = plane_in[root_y]
    send(shape_in.at[my_c], shape_in.at[my_c], 3, device_p(partner))
    for copy in near[:4]:
        copy.wait()
    for way in range(2):
        split_parts(way, near_span.at[way], near_chord.at[way])
    await_all(shape_in.at[0], phase_send.at[3], phase_recv.at[3])
    shape_sum = shape_in[...].reshape(3 * SI, SJ)

    def ring(index, comp, half, forward, step=1):
        later = (index + (step if forward else NY - step)) % NY
        rows = pl.ds(half * (LI // 2), LI // 2)
        way = 0 if forward else 1
        hop = later if forward else NY - later
        return pltpu.make_async_remote_copy(
            src_ref=block.at[index, comp, rows],
            dst_ref=block.at[later, comp, rows],
            send_sem=ring_send.at[way, hop - 1, comp * 2 + half],
            recv_sem=ring_recv.at[way, hop - 1, comp * 2 + half],
            device_id=device_y(step if forward else NY - step),
            device_id_type=MESH,
        )

    sent = []

    def send_ring(index, comp, half, forward, step=1):
        copy = ring(index, comp, half, forward, step)
        copy.start()
        sent.append(copy)

    def hot_rows(index):
        lanes = lax.broadcasted_iota(jnp.int32, (NP * CAP, 3 * LI), 1) % LI
        hot = table_cols[:, index : index + 1] == lanes.astype(jnp.float32)
        return jnp.where(hot, 1.0, 0.0).astype(jnp.bfloat16)

    own = []

    def slots_of(donor):
        return pl.ds(pl.multiple_of((donor * NP + my_p) * CAP, CAP), CAP)

    def choose(index, comp, hot):
        values = block[index, comp]
        high = values.astype(jnp.bfloat16)
        rest = values - high.astype(jnp.float32)
        middle = rest.astype(jnp.bfloat16)
        low = (rest - middle.astype(jnp.float32)).astype(jnp.bfloat16)
        stacked = jnp.concatenate([high, middle, low], axis=0)
        slots = jnp.dot(hot, stacked, preferred_element_type=jnp.float32)
        for peer in range(NP):
            chosen[index, comp, peer] = slots[CAP * peer : CAP * peer + CAP]
        place = slots_of(at_y(NY - index))
        single = index in (3, 4, 5)
        if comp < 2 and not single:
            return
        comps = comp if single else slice(None)
        for peer in peers:
            pltpu.make_async_remote_copy(
                src_ref=chosen.at[index, comps, peer],
                dst_ref=fringe_hbm.at[comps, place],
                send_sem=plane_send,
                recv_sem=plane_recv,
                device_id=device_p(peer),
                device_id_type=MESH,
            ).start()
        if comp == 2:
            copy = pltpu.make_async_copy(
                chosen.at[index, :, my_p], fringe_hbm.at[:, place], self_sem.at[index]
            )
            copy.start()
            own.append(copy)

    parts = [split(shape_sum[comp * SI : (comp + 1) * SI]) for comp in range(3)]
    wide_high = jnp.concatenate([high for high, _ in parts], axis=1)
    wide_low = jnp.concatenate([low for _, low in parts], axis=1)
    wide = jnp.concatenate([wide_high, wide_low, wide_high], axis=0)

    def displaced(index, number, base_of):
        spanwise = lax.dot_general(
            span_parts[number],
            wide,
            (((0,), (0,)), ((), ())),
            preferred_element_type=jnp.float32,
        )
        stacked = jnp.concatenate(
            [spanwise[:, comp * SJ : (comp + 1) * SJ] for comp in range(3)], axis=0
        )
        high, low = split(stacked)
        moved = jnp.dot(
            jnp.concatenate([high, high, low], axis=1),
            chord_parts[number],
            preferred_element_type=jnp.float32,
        )
        for comp in range(3):
            block[index, comp] = base_of[comp] + moved[comp * LI : (comp + 1) * LI]

    for way, index in ((0, 1), (1, NY - 1)):
        near[4 + way].wait()
        displaced(index, way, near_base.at[way])
        for comp in range(3):
            for half in range(2):
                send_ring(index, comp, half, way == 0)
    displaced(0, 2, base)
    for index in (1, NY - 1, 0):
        hot = hot_rows(index)
        for comp in range(3):
            choose(index, comp, hot)

    coords = [block[0, comp] for comp in range(3)]
    along_rows = [dot(op_rows_ref[...], coords[comp]) for comp in range(3)]
    along_cols = [dot(coords[comp], op_cols[...]) for comp in range(3)]
    normal = cross_three(along_rows, along_cols)
    weight = 1.0 + dot_three(normal, normal)
    stream = [flow[comp] for comp in range(3)]
    flux_rows = dot_three(stream, cross_three(along_cols, normal)) / weight
    flux_cols = dot_three(stream, cross_three(normal, along_rows)) / weight
    result[...] = dot(op_rows_ref[...], flux_rows) + dot(flux_cols, op_cols[...])
    leave = pltpu.make_async_copy(result, result_hbm, result_sem)
    leave.start()

    for hop in range(2, NY // 2 + 1):
        last = hop == NY // 2
        hot_up, hot_down = hot_rows(hop), hot_rows(NY - hop)
        for comp in range(3):
            for half in range(2):
                if last:
                    ring(2 if half == 0 else NY - 2, comp, half, half == 0, 2).wait_recv()
                    continue
                ring(hop - 1, comp, half, True).wait_recv()
                if hop < 3:
                    send_ring(hop, comp, half, True)
                if hop == 2 and half == 0:
                    send_ring(hop, comp, half, True, 2)
                ring((NY - hop + 1) % NY, comp, half, False).wait_recv()
                if hop < 3:
                    send_ring(NY - hop, comp, half, False)
                if hop == 2 and half == 1:
                    send_ring(NY - hop, comp, half, False, 2)
            choose(hop, comp, hot_up)
            if not last:
                choose(NY - hop, comp, hot_down)

    for copy in sent:
        copy.wait_send()
    for copy in own:
        copy.wait()
    leave.wait()
    await_all(chosen.at[:, :, pl.ds(0, NP - 1)], plane_send, plane_recv)


def leave(result_in, fringe_in, result_out, fringe_out, sem):
    copies = [
        pltpu.make_async_copy(result_in, result_out, sem.at[0]),
        pltpu.make_async_copy(fringe_in, fringe_out, sem.at[1]),
    ]
    for copy in copies:
        copy.start()
    for copy in copies:
        copy.wait()


def body(
    modal_blocks,
    amplitudes,
    owner_map,
    span_interp,
    chord_interp,
    base_coords,
    flow_state,
    face_rows,
    face_owner,
):
    op_rows = jnp.asarray(compact_operator(LI))
    op_cols = jnp.asarray(np.ascontiguousarray(compact_operator(LJ).T))
    hbm = pl.BlockSpec(memory_space=pltpu.HBM)
    free = pl.BlockSpec(memory_space=pl.ANY)
    f32 = jnp.float32
    result, fringe = pl.pallas_call(
        kernel,
        out_shape=(
            jax.ShapeDtypeStruct((LI, LJ), f32),
            jax.ShapeDtypeStruct((3, NY * NP * CAP, LJ), f32),
        ),
        in_specs=[free] + [hbm] * 10,
        out_specs=(free, free),
        scratch_shapes=[
            pltpu.SMEM((1,), jnp.int32),
            pltpu.SMEM((1, MODES), f32),
            pltpu.VMEM((1, NF), jnp.int32),
            pltpu.VMEM((1, NF), jnp.int32),
            pltpu.VMEM((MODES, 3, SI, SJ), f32),
            pltpu.VMEM((SI, LI), f32),
            pltpu.VMEM((SJ, LJ), f32),
            pltpu.VMEM((3, LI, LJ), f32),
            pltpu.VMEM((3, LI, LJ), f32),
            pltpu.VMEM((LI, LI), f32),
            pltpu.VMEM((LJ, LJ), f32),
            pltpu.VMEM((2, SI, LI), f32),
            pltpu.VMEM((2, SJ, LJ), f32),
            pltpu.VMEM((2, 3, LI, LJ), f32),
            pltpu.VMEM((3, 3 * SI, LI), jnp.bfloat16),
            pltpu.VMEM((3, 3 * SJ, LJ), jnp.bfloat16),
            pltpu.VMEM((LI, LJ), f32),
            pltpu.VMEM((NC, 3 * SI // NC, SJ), f32),
            pltpu.VMEM((NC, 3 * SI // NC, SJ), f32),
            pltpu.VMEM((NP // NC, 3 * SI // NC, SJ), f32),
            pltpu.VMEM((NY, 3 * SI // NC, SJ), f32),
            pltpu.VMEM((NC, 3 * SI // NC, SJ), f32),
            pltpu.VMEM((1, NY * NP * CAP), f32),
            pltpu.VMEM((NY, 1, NY * NP * CAP), f32),
            pltpu.VMEM((NY, 3, LI, LJ), f32),
            pltpu.VMEM((NY, 3, NP, CAP, LJ), f32),
            pltpu.SemaphoreType.DMA((11,)),
            pltpu.SemaphoreType.DMA((4,)),
            pltpu.SemaphoreType.DMA((4,)),
            pltpu.SemaphoreType.DMA,
            pltpu.SemaphoreType.DMA,
            pltpu.SemaphoreType.DMA((2, 4, 6)),
            pltpu.SemaphoreType.DMA((2, 4, 6)),
            pltpu.SemaphoreType.DMA,
            pltpu.SemaphoreType.DMA,
            pltpu.SemaphoreType.DMA((NY,)),
            pltpu.SemaphoreType.DMA,
            pltpu.SemaphoreType.DMA((2, 3)),
            pltpu.SemaphoreType.DMA((2, 3)),
        ],
        compiler_params=pltpu.CompilerParams(collective_id=0, has_side_effects=True, vmem_limit_bytes=12 << 20),
        name="section",
    )(
        owner_map,
        *(
            pltpu.with_memory_space_constraint(array, pltpu.HBM)
            for array in (
                amplitudes,
                face_rows,
                face_owner.reshape(1, NF),
                modal_blocks[0],
                span_interp[0],
                chord_interp[0],
                base_coords[0],
                flow_state[0],
                op_rows,
                op_cols,
            )
        ),
    )
    result, fringe = pl.pallas_call(
        leave,
        out_shape=(
            jax.ShapeDtypeStruct(result.shape, f32),
            jax.ShapeDtypeStruct(fringe.shape, f32),
        ),
        in_specs=[free, free],
        out_specs=(hbm, hbm),
        scratch_shapes=[pltpu.SemaphoreType.DMA((2,))],
        compiler_params=pltpu.CompilerParams(vmem_limit_bytes=1 << 20),
        name="leave",
    )(result, fringe)
    return (result[None], fringe.transpose(1, 0, 2)[None])


def solution(mesh):
    return jax.shard_map(
        body,
        mesh=mesh,
        in_specs=(
            P("blade", "grid", None, None, None),
            P("blade", None),
            P("blade"),
            P("blade", None, "grid"),
            P("blade", "grid", None),
            P("blade", None, "grid", None),
            P("blade", None, "grid", None),
            P("blade", "grid"),
            P("blade", "grid", None),
        ),
        out_specs=(P("blade", "grid", None), P("blade", "grid", None, None)),
        check_vma=False,
    )
```
